128 devices in a mesh: ifg: 32 (over y, x_lo, z), rows: 4 (over x_hi, core).
Axes of the slice: x: 4 (x_hi: 2, x_lo: 2; x = x_hi * 2 + x_lo), y: 4, z: 4, core: 2. Of those that a mesh axis runs over, the one named last changes fastest.
Arguments:
- phase: float32 [256, 128, 2048], P('ifg', 'rows'), may hold values from -3.1416 to 3.1416, as said below
- weights: int32 [256, 128, 2048], P('ifg', 'rows'), may hold values from 1 to 16
- network: int32 [256, 2], replicated, may hold values from 0 to 95, as said below
Outputs:
- series: float32 [95, 128, 2048], P(None, 'rows', 'ifg')
- filtered: bfloat16 [256, 128, 2048], P(None, 'rows', 'ifg')
The draws below stay inside these ranges and needn't reach their ends.
Inputs may be any that keep to these rules, and one draw needn't show every extreme that they name: `phase`: values lie in the range of atan2. `network`: row e < 95 joins date e to date e + 1; every row names an earlier date in column 0 and a later date in column 1, at most 24 dates apart, and the span 24 occurs.
All inputs are finite; a program needn't handle non-finite values.
Results may differ from the reference program's by a relative error of at most 0.0018.
Values sent between devices are 32-bit elements; how exact they have to be, the bound alone decides.
A program may use at most 192 MiB of HBM per device.

```python
import jax
import jax.numpy as jnp
from jax import lax

IFG = 256
DATES = 96
W = 2048
SWEEPS = 4
SPAN = 24
H = 128
EPOCHS = 95


def network_pairs(key):
    keys = jax.random.split(jax.random.fold_in(key, 11), 2)
    extra = IFG - EPOCHS
    spans = jax.random.randint(keys[0], (extra,), 1, SPAN + 1)
    spans = spans.at[0].set(SPAN)
    starts = jax.random.randint(keys[1], (extra,), 0, DATES - spans)
    chain = jnp.arange(EPOCHS, dtype=jnp.int32)
    earlier = jnp.concatenate([chain, starts.astype(jnp.int32)])
    later_date = jnp.concatenate([chain + 1, (starts + spans).astype(jnp.int32)])
    return jnp.stack([earlier, later_date], axis=1).astype(jnp.int32)


def date_field(params, index, row_pos, col_pos):
    amp_one, rate_r1, rate_c1, off_one, amp_two, rate_r2, rate_c2, off_two = [p[index][:, None, None] for p in params]
    first = amp_one * jnp.sin(rate_r1 * row_pos + rate_c1 * col_pos + off_one)
    second = amp_two * jnp.cos(rate_r2 * row_pos + rate_c2 * col_pos + off_two)
    return first + second


def draw_phase(key, part):
    pairs = network_pairs(key)
    keys = jax.random.split(jax.random.fold_in(key, 23), 9)
    amp_most = 1.0
    noise_most = 0.5
    params = [jax.random.uniform(keys[0], (DATES,), jnp.float32, 0.2, amp_most), jax.random.uniform(keys[1], (DATES,), jnp.float32, -0.15, 0.15), jax.random.uniform(keys[2], (DATES,), jnp.float32, -0.15, 0.15), jax.random.uniform(keys[3], (DATES,), jnp.float32, 0.0, 6.2831), jax.random.uniform(keys[4], (DATES,), jnp.float32, 0.2, amp_most), jax.random.uniform(keys[5], (DATES,), jnp.float32, -0.05, 0.05), jax.random.uniform(keys[6], (DATES,), jnp.float32, -0.05, 0.05), jax.random.uniform(keys[7], (DATES,), jnp.float32, 0.0, 6.2831)]
    row_pos = jnp.arange(H, dtype=jnp.float32)[None, :, None]
    col_pos = jnp.arange(W, dtype=jnp.float32)[None, None, :]
    later_part = date_field(params, pairs[:, 1], row_pos, col_pos)
    earlier_part = date_field(params, pairs[:, 0], row_pos, col_pos)
    noise = jax.random.uniform(keys[8], (IFG, H, W), jnp.float32, -noise_most, noise_most)
    truth = later_part - earlier_part + noise
    return jnp.arctan2(jnp.sin(truth), jnp.cos(truth)).astype(jnp.float32)


def draw_network(key, part):
    return network_pairs(key)


def plant(drawn, rng, smallest, largest):
    index_at = [jax.random.randint(jax.random.fold_in(rng, axis), (), 0, length) for axis, length in enumerate(drawn.shape)]
    main_axis = drawn.shape.index(max(drawn.shape))
    neighbour = index_at[:main_axis] + [(index_at[main_axis] + 1) % drawn.shape[main_axis]] + index_at[main_axis + 1:]
    return drawn.at[tuple(index_at)].set(smallest).at[tuple(neighbour)].set(largest)


def setup_inputs(seed: int = 0) -> dict:
    arg_keys = jax.random.split(jax.random.key(seed), 4)
    phase = draw_phase(jax.random.fold_in(arg_keys[3], 71), 0)
    weights = plant(jax.random.randint(arg_keys[1], (IFG, H, W), 1, 17), jax.random.fold_in(arg_keys[1], 1), 1, 16).astype(jnp.int32)
    network = draw_network(jax.random.fold_in(arg_keys[3], 71), 0)
    return dict(phase=phase, weights=weights, network=network)


def wrapped_diff(delta):
    return jnp.arctan2(jnp.sin(delta), jnp.cos(delta))

def edge_terms(phase_ext, quality_ext):
    grad_rows = wrapped_diff(phase_ext[:, 1:] - phase_ext[:, :-1])
    weight_rows = quality_ext[:, 1:] * quality_ext[:, :-1]
    grad_horiz = wrapped_diff(phase_ext[:, :, 1:] - phase_ext[:, :, :-1])
    weight_horiz = quality_ext[:, :, 1:] * quality_ext[:, :, :-1]
    widths = ((0, 0), (0, 0), (1, 1))
    return (grad_rows, weight_rows, jnp.pad(grad_horiz, widths), jnp.pad(weight_horiz, widths))

def jacobi_sweep(current, grad_rows, weight_rows, grad_cols, weight_cols, floored):
    padded_cols = jnp.pad(current, ((0, 0), (0, 0), (1, 1)))
    numerator = weight_rows[:, :-1] * (current[:, :-2] + grad_rows[:, :-1])
    numerator = numerator + weight_rows[:, 1:] * (current[:, 2:] - grad_rows[:, 1:])
    numerator = numerator + weight_cols[:, 1:-1, :-1] * (padded_cols[:, 1:-1, :-2] + grad_cols[:, 1:-1, :-1])
    numerator = numerator + weight_cols[:, 1:-1, 1:] * (padded_cols[:, 1:-1, 2:] - grad_cols[:, 1:-1, 1:])
    denominator = weight_rows[:, :-1] + weight_rows[:, 1:]
    denominator = denominator + weight_cols[:, 1:-1, :-1] + weight_cols[:, 1:-1, 1:]
    if floored:
        denominator = jnp.where(denominator > 0.0, denominator, 1.0)
    return numerator / denominator

def binomial(padded, axis):
    length = padded.shape[axis] - 4

    def shifted(offset):
        return lax.slice_in_dim(padded, offset, offset + length, axis=axis)
    return (shifted(0) + 4.0 * shifted(1) + 6.0 * shifted(2) + 4.0 * shifted(3) + shifted(4)) * 0.0625

def network_maps(network):
    date_ids = jnp.arange(DATES, dtype=jnp.int32)[None, :]
    full = (network[:, 1:2] == date_ids).astype(jnp.float32) - (network[:, 0:1] == date_ids).astype(jnp.float32)
    design = full[:, 1:]
    normal_matrix = jnp.dot(design.T, design, precision=lax.Precision.HIGHEST)
    factor = jnp.linalg.cholesky(normal_matrix)
    pseudo = jax.scipy.linalg.cho_solve((factor, True), design.T)
    return (design, pseudo)

def reference(phase, weights, network):
    design, pseudo = network_maps(network)
    rim = ((0, 0), (1, 1), (0, 0))

    def unwrap_one(pair):
        phase_one, weight_one = pair
        phase_one = phase_one[None]
        quality = weight_one.astype(jnp.float32)[None]
        grad_rows, weight_rows, grad_cols, weight_cols = edge_terms(jnp.pad(phase_one, rim), jnp.pad(quality, rim))
        current = jnp.zeros_like(phase_one)
        for sweep_index in range(SWEEPS):
            current = jacobi_sweep(jnp.pad(current, rim), grad_rows, weight_rows, grad_cols, weight_cols, False)
        return current[0]
    unwrapped = lax.map(unwrap_one, (phase, weights))
    series = jnp.einsum('ei,irc->erc', pseudo, unwrapped, precision=lax.Precision.HIGHEST)
    residual = unwrapped - jnp.einsum('ie,erc->irc', design, series, precision=lax.Precision.HIGHEST)

    def smooth_one(plane):
        rows_done = binomial(jnp.pad(plane, ((2, 2), (0, 0))), 0)
        return binomial(jnp.pad(rows_done, ((0, 0), (2, 2))), 1).astype(jnp.bfloat16)
    filtered = lax.map(smooth_one, residual)
    return (series, filtered)
```

```python
import jax
import jax.numpy as jnp
from jax import lax
from jax.sharding import PartitionSpec as P

DATES = 96
SWEEPS = 4
HALO = SWEEPS


def extended_2(block, sides, width):
    for axis, dim in sides:
        count = lax.axis_size(axis)
        forward = [(i, i + 1) for i in range(count - 1)]
        backward = [(target, source) for source, target in forward]
        low = lax.ppermute(
            lax.slice_in_dim(block, block.shape[dim] - width, None, axis=dim), axis, forward
        )
        high = lax.ppermute(lax.slice_in_dim(block, 0, width, axis=dim), axis, backward)
        block = jnp.concatenate([low, block, high], axis=dim)
    return block


def wrapped_diff(delta):
    return jnp.arctan2(jnp.sin(delta), jnp.cos(delta))


def edge_terms(phase_ext, quality_ext):
    grad_rows = wrapped_diff(phase_ext[:, 1:] - phase_ext[:, :-1])
    weight_rows = quality_ext[:, 1:] * quality_ext[:, :-1]
    grad_horiz = wrapped_diff(phase_ext[:, :, 1:] - phase_ext[:, :, :-1])
    weight_horiz = quality_ext[:, :, 1:] * quality_ext[:, :, :-1]
    widths = ((0, 0), (0, 0), (1, 1))
    return (grad_rows, weight_rows, jnp.pad(grad_horiz, widths), jnp.pad(weight_horiz, widths))


def jacobi_sweep(current, grad_rows, weight_rows, grad_cols, weight_cols):
    padded_cols = jnp.pad(current, ((0, 0), (0, 0), (1, 1)))
    numerator = weight_rows[:, :-1] * (current[:, :-2] + grad_rows[:, :-1])
    numerator = numerator + weight_rows[:, 1:] * (current[:, 2:] - grad_rows[:, 1:])
    numerator = numerator + weight_cols[:, 1:-1, :-1] * (
        padded_cols[:, 1:-1, :-2] + grad_cols[:, 1:-1, :-1]
    )
    numerator = numerator + weight_cols[:, 1:-1, 1:] * (
        padded_cols[:, 1:-1, 2:] - grad_cols[:, 1:-1, 1:]
    )
    denominator = weight_rows[:, :-1] + weight_rows[:, 1:]
    denominator = denominator + weight_cols[:, 1:-1, :-1] + weight_cols[:, 1:-1, 1:]
    denominator = jnp.where(denominator > 0.0, denominator, 1.0)
    return numerator / denominator


def binomial(padded, axis):
    length = padded.shape[axis] - 4

    def shifted(offset):
        return lax.slice_in_dim(padded, offset, offset + length, axis=axis)

    return (
        shifted(0) + 4.0 * shifted(1) + 6.0 * shifted(2) + 4.0 * shifted(3) + shifted(4)
    ) * 0.0625


def network_maps(network):
    date_ids = jnp.arange(DATES, dtype=jnp.int32)[None, :]
    full = (network[:, 1:2] == date_ids).astype(jnp.float32) - (network[:, 0:1] == date_ids).astype(
        jnp.float32
    )
    design = full[:, 1:]
    normal_matrix = jnp.dot(design.T, design, precision=lax.Precision.HIGHEST)
    factor = jnp.linalg.cholesky(normal_matrix)
    pseudo = jax.scipy.linalg.cho_solve((factor, True), design.T)
    return (design, pseudo)


def on_device(phase, weights, network):
    design, pseudo = network_maps(network)
    stacked = jnp.stack([phase, weights.astype(jnp.float32)])
    extended = extended_2(stacked, (("rows", 2),), HALO)
    rim = ((0, 0), (1, 1), (0, 0))
    grad_rows, weight_rows, grad_cols, weight_cols = edge_terms(
        jnp.pad(extended[0], rim), jnp.pad(extended[1], rim)
    )
    current = jnp.zeros_like(extended[0])
    for sweep_index in range(SWEEPS):
        current = jacobi_sweep(jnp.pad(current, rim), grad_rows, weight_rows, grad_cols, weight_cols)
    current = current[:, HALO:-HALO]
    block = lax.all_to_all(current, "ifg", split_axis=2, concat_axis=0, tiled=True)
    series_block = jnp.einsum("ei,irc->erc", pseudo, block, precision=lax.Precision.HIGHEST)
    residual = block - jnp.einsum(
        "ie,erc->irc", design, series_block, precision=lax.Precision.HIGHEST
    )
    padded = extended_2(residual, (("rows", 1), ("ifg", 2)), 2)
    filtered = binomial(binomial(padded, 1), 2)
    return (series_block, filtered.astype(jnp.bfloat16))


def solution(mesh):
    return jax.shard_map(
        on_device,
        mesh=mesh,
        in_specs=(P("ifg", "rows", None), P("ifg", "rows", None), P()),
        out_specs=(P(None, "rows", "ifg"), P(None, "rows", "ifg")),
        check_vma=False,
    )
```

```python
import functools

import numpy as np
import jax
import jax.numpy as jnp
from jax import lax
from jax.experimental import pallas as pl
from jax.experimental.pallas import tpu as pltpu
from jax.sharding import PartitionSpec as P

DATES = 96
SWEEPS = 4
HALO = SWEEPS
PI32 = float(np.float32(np.pi))
TWO_PI_HI = float(np.float32(2 * np.pi))
TWO_PI_LO = float(np.float32(2 * np.pi - np.float64(np.float32(2 * np.pi))))


def extended_2(block, sides, width):
    for axis, dim in sides:
        count = lax.axis_size(axis)
        forward = [(i, i + 1) for i in range(count - 1)]
        backward = [(target, source) for source, target in forward]
        low = lax.ppermute(
            lax.slice_in_dim(block, block.shape[dim] - width, None, axis=dim), axis, forward
        )
        high = lax.ppermute(lax.slice_in_dim(block, 0, width, axis=dim), axis, backward)
        block = jnp.concatenate([low, block, high], axis=dim)
    return block


def wrapped_diff(delta):
    above = (delta - TWO_PI_HI) - TWO_PI_LO
    below = (delta + TWO_PI_HI) + TWO_PI_LO
    return jnp.where(delta >= PI32, above, jnp.where(delta <= -PI32, below, delta))


def unwrap_kernel(rows_out, p_ref, q_ref, o_ref, cur_ref):
    p = p_ref[0]
    q = q_ref[0]
    nr, nc = p.shape
    row = lax.broadcasted_iota(jnp.int32, (nr, nc), 0)
    col = lax.broadcasted_iota(jnp.int32, (nr, nc), 1)
    zero = jnp.zeros((nr, nc), jnp.float32)
    p_dn = pltpu.roll(p, nr - 1, 0)
    q_dn = pltpu.roll(q, nr - 1, 0)
    g_dn = wrapped_diff(p_dn - p)
    w_dn = jnp.where(row < nr - 1, q_dn * q, zero)
    p_rt = pltpu.roll(p, nc - 1, 1)
    q_rt = pltpu.roll(q, nc - 1, 1)
    g_rt = wrapped_diff(p_rt - p)
    w_rt = jnp.where(col < nc - 1, q_rt * q, zero)
    g_up = pltpu.roll(g_dn, 1, 0)
    w_up = pltpu.roll(w_dn, 1, 0)
    g_lt = pltpu.roll(g_rt, 1, 1)
    w_lt = pltpu.roll(w_rt, 1, 1)
    den = ((w_up + w_dn) + w_lt) + w_rt
    den = jnp.where(den > 0.0, den, 1.0)
    cur = zero
    for _ in range(SWEEPS):
        c_up = pltpu.roll(cur, 1, 0)
        c_dn = pltpu.roll(cur, nr - 1, 0)
        c_lt = pltpu.roll(cur, 1, 1)
        c_rt = pltpu.roll(cur, nc - 1, 1)
        num = w_up * (c_up + g_up)
        num = num + w_dn * (c_dn - g_dn)
        num = num + w_lt * (c_lt + g_lt)
        num = num + w_rt * (c_rt - g_rt)
        cur = num / den
    cur_ref[...] = cur
    o_ref[0] = cur_ref[pl.ds(HALO, rows_out), :]


def unwrap(phase_ext, quality_ext, rows_out):
    n, nr, nc = phase_ext.shape
    return pl.pallas_call(
        functools.partial(unwrap_kernel, rows_out),
        grid=(n,),
        in_specs=[
            pl.BlockSpec((1, nr, nc), lambda i: (i, 0, 0)),
            pl.BlockSpec((1, nr, nc), lambda i: (i, 0, 0)),
        ],
        out_specs=pl.BlockSpec((1, rows_out, nc), lambda i: (i, 0, 0)),
        out_shape=jax.ShapeDtypeStruct((n, rows_out, nc), jnp.float32),
        scratch_shapes=[pltpu.VMEM((nr, nc), jnp.float32)],
        cost_estimate=pl.CostEstimate(
            flops=120 * n * nr * nc, bytes_accessed=4 * n * nc * (2 * nr + rows_out), transcendentals=0
        ),
    )(phase_ext, quality_ext)


def binomial(padded, axis):
    length = padded.shape[axis] - 4

    def shifted(offset):
        return lax.slice_in_dim(padded, offset, offset + length, axis=axis)

    return (
        shifted(0) + 4.0 * shifted(1) + 6.0 * shifted(2) + 4.0 * shifted(3) + shifted(4)
    ) * 0.0625


def network_maps(network):
    date_ids = jnp.arange(DATES, dtype=jnp.int32)[None, :]
    full = (network[:, 1:2] == date_ids).astype(jnp.float32) - (network[:, 0:1] == date_ids).astype(
        jnp.float32
    )
    design = full[:, 1:]
    normal_matrix = jnp.dot(design.T, design, precision=lax.Precision.HIGHEST)
    factor = jnp.linalg.cholesky(normal_matrix)
    pseudo = jax.scipy.linalg.cho_solve((factor, True), design.T)
    return (design, pseudo)


def on_device(phase, weights, network):
    design, pseudo = network_maps(network)
    stacked = jnp.stack([phase, weights.astype(jnp.float32)])
    extended = extended_2(stacked, (("rows", 2),), HALO)
    current = unwrap(extended[0], extended[1], phase.shape[1])
    block = lax.all_to_all(current, "ifg", split_axis=2, concat_axis=0, tiled=True)
    series_block = jnp.einsum("ei,irc->erc", pseudo, block, precision=lax.Precision.HIGHEST)
    residual = block - jnp.einsum(
        "ie,erc->irc", design, series_block, precision=lax.Precision.HIGHEST
    )
    padded = extended_2(residual, (("rows", 1), ("ifg", 2)), 2)
    filtered = binomial(binomial(padded, 1), 2)
    return (series_block, filtered.astype(jnp.bfloat16))


def solution(mesh):
    return jax.shard_map(
        on_device,
        mesh=mesh,
        in_specs=(P("ifg", "rows", None), P("ifg", "rows", None), P()),
        out_specs=(P(None, "rows", "ifg"), P(None, "rows", "ifg")),
        check_vma=False,
    )
```

```python
import functools

import numpy as np
import jax
import jax.numpy as jnp
from jax import lax
from jax.experimental import pallas as pl
from jax.experimental.pallas import tpu as pltpu
from jax.sharding import PartitionSpec as P

DATES = 96
SWEEPS = 4
HALO = SWEEPS
PI32 = float(np.float32(np.pi))
TWO_PI_HI = float(np.float32(2 * np.pi))
TWO_PI_LO = float(np.float32(2 * np.pi - np.float64(np.float32(2 * np.pi))))


def extended_2(block, sides, width):
    for axis, dim in sides:
        count = lax.axis_size(axis)
        forward = [(i, i + 1) for i in range(count - 1)]
        backward = [(target, source) for source, target in forward]
        low = lax.ppermute(
            lax.slice_in_dim(block, block.shape[dim] - width, None, axis=dim), axis, forward
        )
        high = lax.ppermute(lax.slice_in_dim(block, 0, width, axis=dim), axis, backward)
        block = jnp.concatenate([low, block, high], axis=dim)
    return block


def wrapped_diff(delta):
    above = (delta - TWO_PI_HI) - TWO_PI_LO
    below = (delta + TWO_PI_HI) + TWO_PI_LO
    return jnp.where(delta >= PI32, above, jnp.where(delta <= -PI32, below, delta))


def unwrap_kernel(rows_out, p_ref, q_ref, o_ref, cur_ref):
    p = p_ref[0]
    q = q_ref[0]
    nr, nc = p.shape
    row = lax.broadcasted_iota(jnp.int32, (nr, nc), 0)
    col = lax.broadcasted_iota(jnp.int32, (nr, nc), 1)
    zero = jnp.zeros((nr, nc), jnp.float32)
    p_dn = pltpu.roll(p, nr - 1, 0)
    q_dn = pltpu.roll(q, nr - 1, 0)
    g_dn = wrapped_diff(p_dn - p)
    w_dn = jnp.where(row < nr - 1, q_dn * q, zero)
    p_rt = pltpu.roll(p, nc - 1, 1)
    q_rt = pltpu.roll(q, nc - 1, 1)
    g_rt = wrapped_diff(p_rt - p)
    w_rt = jnp.where(col < nc - 1, q_rt * q, zero)
    g_up = pltpu.roll(g_dn, 1, 0)
    w_up = pltpu.roll(w_dn, 1, 0)
    g_lt = pltpu.roll(g_rt, 1, 1)
    w_lt = pltpu.roll(w_rt, 1, 1)
    den = ((w_up + w_dn) + w_lt) + w_rt
    den = jnp.where(den > 0.0, den, 1.0)
    cur = zero
    for _ in range(SWEEPS):
        c_up = pltpu.roll(cur, 1, 0)
        c_dn = pltpu.roll(cur, nr - 1, 0)
        c_lt = pltpu.roll(cur, 1, 1)
        c_rt = pltpu.roll(cur, nc - 1, 1)
        num = w_up * (c_up + g_up)
        num = num + w_dn * (c_dn - g_dn)
        num = num + w_lt * (c_lt + g_lt)
        num = num + w_rt * (c_rt - g_rt)
        cur = num / den
    cur_ref[...] = cur
    half = rows_out // 2
    upper = cur_ref[pl.ds(HALO, half), :]
    lower = cur_ref[pl.ds(HALO + half, half), :]
    lane = lax.broadcasted_iota(jnp.int32, (half, nc), 1) % 128
    first = lane < 64
    even = jnp.where(first, upper, pltpu.roll(lower, 64, 1))
    odd = jnp.where(first, pltpu.roll(upper, nc - 64, 1), lower)
    for m in range(nc // 128):
        o_ref[2 * m, 0] = even[:, 128 * m : 128 * (m + 1)]
        o_ref[2 * m + 1, 0] = odd[:, 128 * m : 128 * (m + 1)]


def unwrap(phase_ext, quality_ext, rows_out):
    n, nr, nc = phase_ext.shape
    return pl.pallas_call(
        functools.partial(unwrap_kernel, rows_out),
        grid=(n,),
        in_specs=[
            pl.BlockSpec((1, nr, nc), lambda i: (i, 0, 0)),
            pl.BlockSpec((1, nr, nc), lambda i: (i, 0, 0)),
        ],
        out_specs=pl.BlockSpec((nc // 64, 1, rows_out // 2, 128), lambda i: (0, i, 0, 0)),
        out_shape=jax.ShapeDtypeStruct((nc // 64, n, rows_out // 2, 128), jnp.float32),
        scratch_shapes=[pltpu.VMEM((nr, nc), jnp.float32)],
        cost_estimate=pl.CostEstimate(
            flops=120 * n * nr * nc, bytes_accessed=4 * n * nc * (2 * nr + rows_out), transcendentals=0
        ),
    )(phase_ext, quality_ext)


def binomial(padded, axis):
    length = padded.shape[axis] - 4

    def shifted(offset):
        return lax.slice_in_dim(padded, offset, offset + length, axis=axis)

    return (
        shifted(0) + 4.0 * shifted(1) + 6.0 * shifted(2) + 4.0 * shifted(3) + shifted(4)
    ) * 0.0625


def network_maps(network):
    date_ids = jnp.arange(DATES, dtype=jnp.int32)[None, :]
    full = (network[:, 1:2] == date_ids).astype(jnp.float32) - (network[:, 0:1] == date_ids).astype(
        jnp.float32
    )
    design = full[:, 1:]
    normal_matrix = jnp.dot(design.T, design, precision=lax.Precision.HIGHEST)
    factor = jnp.linalg.cholesky(normal_matrix)
    pseudo = jax.scipy.linalg.cho_solve((factor, True), design.T)
    return (design, pseudo)


def on_device(phase, weights, network):
    design, pseudo = network_maps(network)
    stacked = jnp.stack([phase, weights.astype(jnp.float32)])
    extended = extended_2(stacked, (("rows", 2),), HALO)
    rows = phase.shape[1]
    current = unwrap(extended[0], extended[1], rows)
    received = lax.all_to_all(current, "ifg", split_axis=0, concat_axis=0, tiled=True)
    ifg = received.shape[0] * received.shape[1]
    block = received.reshape(ifg, rows // 2, 2, 64).transpose(0, 2, 1, 3).reshape(ifg, rows, 64)
    series_block = jnp.einsum("ei,irc->erc", pseudo, block, precision=lax.Precision.HIGHEST)
    residual = block - jnp.einsum(
        "ie,erc->irc", design, series_block, precision=lax.Precision.HIGHEST
    )
    padded = extended_2(residual, (("rows", 1), ("ifg", 2)), 2)
    filtered = binomial(binomial(padded, 1), 2)
    return (series_block, filtered.astype(jnp.bfloat16))


def solution(mesh):
    return jax.shard_map(
        on_device,
        mesh=mesh,
        in_specs=(P("ifg", "rows", None), P("ifg", "rows", None), P()),
        out_specs=(P(None, "rows", "ifg"), P(None, "rows", "ifg")),
        check_vma=False,
    )
```

```python
import functools

import numpy as np
import jax
import jax.numpy as jnp
from jax import lax
from jax.experimental import pallas as pl
from jax.experimental.pallas import tpu as pltpu
from jax.sharding import PartitionSpec as P

DATES = 96
SWEEPS = 4
HALO = SWEEPS
PI32 = float(np.float32(np.pi))
TWO_PI_HI = float(np.float32(2 * np.pi))
TWO_PI_LO = float(np.float32(2 * np.pi - np.float64(np.float32(2 * np.pi))))


def extended_2(block, sides, width):
    for axis, dim in sides:
        count = lax.axis_size(axis)
        forward = [(i, i + 1) for i in range(count - 1)]
        backward = [(target, source) for source, target in forward]
        low = lax.ppermute(
            lax.slice_in_dim(block, block.shape[dim] - width, None, axis=dim), axis, forward
        )
        high = lax.ppermute(lax.slice_in_dim(block, 0, width, axis=dim), axis, backward)
        block = jnp.concatenate([low, block, high], axis=dim)
    return block


def halo_2d(block, width):
    nrows, nifg = lax.axis_size("rows"), lax.axis_size("ifg")
    end_r, end_c = block.shape[1] - width, block.shape[2] - width

    def send(part, step_r, step_i):
        pairs = []
        for i in range(nifg):
            for r in range(nrows):
                ti, tr = i + step_i, r + step_r
                if 0 <= ti < nifg and 0 <= tr < nrows:
                    pairs.append((i * nrows + r, ti * nrows + tr))
        return lax.ppermute(part, ("ifg", "rows"), pairs)

    top, bottom = block[:, end_r:], block[:, :width]
    upper = jnp.concatenate(
        [send(top[:, :, end_c:], 1, 1), send(top, 1, 0), send(top[:, :, :width], 1, -1)], axis=2
    )
    middle = jnp.concatenate(
        [send(block[:, :, end_c:], 0, 1), block, send(block[:, :, :width], 0, -1)], axis=2
    )
    lower = jnp.concatenate(
        [send(bottom[:, :, end_c:], -1, 1), send(bottom, -1, 0), send(bottom[:, :, :width], -1, -1)],
        axis=2,
    )
    return jnp.concatenate([upper, middle, lower], axis=1)


def wrapped_diff(delta):
    above = (delta - TWO_PI_HI) - TWO_PI_LO
    below = (delta + TWO_PI_HI) + TWO_PI_LO
    return jnp.where(delta >= PI32, above, jnp.where(delta <= -PI32, below, delta))


def unwrap_kernel(rows_out, p_ref, q_ref, o_ref, cur_ref):
    p = p_ref[0]
    q = q_ref[0]
    nr, nc = p.shape
    row = lax.broadcasted_iota(jnp.int32, (nr, nc), 0)
    col = lax.broadcasted_iota(jnp.int32, (nr, nc), 1)
    zero = jnp.zeros((nr, nc), jnp.float32)
    p_dn = pltpu.roll(p, nr - 1, 0)
    q_dn = pltpu.roll(q, nr - 1, 0)
    g_dn = wrapped_diff(p_dn - p)
    w_dn = jnp.where(row < nr - 1, q_dn * q, zero)
    p_rt = pltpu.roll(p, nc - 1, 1)
    q_rt = pltpu.roll(q, nc - 1, 1)
    g_rt = wrapped_diff(p_rt - p)
    w_rt = jnp.where(col < nc - 1, q_rt * q, zero)
    g_up = pltpu.roll(g_dn, 1, 0)
    w_up = pltpu.roll(w_dn, 1, 0)
    g_lt = pltpu.roll(g_rt, 1, 1)
    w_lt = pltpu.roll(w_rt, 1, 1)
    den = ((w_up + w_dn) + w_lt) + w_rt
    den = jnp.where(den > 0.0, den, 1.0)
    cur = zero
    for _ in range(SWEEPS):
        c_up = pltpu.roll(cur, 1, 0)
        c_dn = pltpu.roll(cur, nr - 1, 0)
        c_lt = pltpu.roll(cur, 1, 1)
        c_rt = pltpu.roll(cur, nc - 1, 1)
        num = w_up * (c_up + g_up)
        num = num + w_dn * (c_dn - g_dn)
        num = num + w_lt * (c_lt + g_lt)
        num = num + w_rt * (c_rt - g_rt)
        cur = num / den
    cur_ref[...] = cur
    half = rows_out // 2
    upper = cur_ref[pl.ds(HALO, half), :]
    lower = cur_ref[pl.ds(HALO + half, half), :]
    lane = lax.broadcasted_iota(jnp.int32, (half, nc), 1) % 128
    first = lane < 64
    even = jnp.where(first, upper, pltpu.roll(lower, 64, 1))
    odd = jnp.where(first, pltpu.roll(upper, nc - 64, 1), lower)
    for m in range(nc // 128):
        o_ref[2 * m, 0] = even[:, 128 * m : 128 * (m + 1)]
        o_ref[2 * m + 1, 0] = odd[:, 128 * m : 128 * (m + 1)]


def unwrap(phase_ext, quality_ext, rows_out):
    n, nr, nc = phase_ext.shape
    return pl.pallas_call(
        functools.partial(unwrap_kernel, rows_out),
        grid=(n,),
        in_specs=[
            pl.BlockSpec((1, nr, nc), lambda i: (i, 0, 0)),
            pl.BlockSpec((1, nr, nc), lambda i: (i, 0, 0)),
        ],
        out_specs=pl.BlockSpec((nc // 64, 1, rows_out // 2, 128), lambda i: (0, i, 0, 0)),
        out_shape=jax.ShapeDtypeStruct((nc // 64, n, rows_out // 2, 128), jnp.float32),
        scratch_shapes=[pltpu.VMEM((nr, nc), jnp.float32)],
        cost_estimate=pl.CostEstimate(
            flops=120 * n * nr * nc, bytes_accessed=4 * n * nc * (2 * nr + rows_out), transcendentals=0
        ),
    )(phase_ext, quality_ext)


def binomial(padded, axis):
    length = padded.shape[axis] - 4

    def shifted(offset):
        return lax.slice_in_dim(padded, offset, offset + length, axis=axis)

    return (
        shifted(0) + 4.0 * shifted(1) + 6.0 * shifted(2) + 4.0 * shifted(3) + shifted(4)
    ) * 0.0625


def network_maps(network):
    date_ids = jnp.arange(DATES, dtype=jnp.int32)[None, :]
    full = (network[:, 1:2] == date_ids).astype(jnp.float32) - (network[:, 0:1] == date_ids).astype(
        jnp.float32
    )
    design = full[:, 1:]
    normal_matrix = jnp.dot(design.T, design, precision=lax.Precision.HIGHEST)
    factor = jnp.linalg.cholesky(normal_matrix)
    pseudo = jax.scipy.linalg.cho_solve((factor, True), design.T)
    return (design, pseudo)


def on_device(phase, weights, network):
    design, pseudo = network_maps(network)
    stacked = jnp.stack([phase, weights.astype(jnp.float32)])
    extended = extended_2(stacked, (("rows", 2),), HALO)
    rows = phase.shape[1]
    current = unwrap(extended[0], extended[1], rows)
    received = lax.all_to_all(current, "ifg", split_axis=0, concat_axis=0, tiled=True)
    ifg = received.shape[0] * received.shape[1]
    block = received.reshape(ifg, rows // 2, 2, 64).transpose(0, 2, 1, 3).reshape(ifg, rows, 64)
    series_block = jnp.einsum("ei,irc->erc", pseudo, block, precision=lax.Precision.HIGHEST)
    residual = block - jnp.einsum(
        "ie,erc->irc", design, series_block, precision=lax.Precision.HIGHEST
    )
    padded = halo_2d(residual, 2)
    filtered = binomial(binomial(padded, 1), 2)
    return (series_block, filtered.astype(jnp.bfloat16))


def solution(mesh):
    return jax.shard_map(
        on_device,
        mesh=mesh,
        in_specs=(P("ifg", "rows", None), P("ifg", "rows", None), P()),
        out_specs=(P(None, "rows", "ifg"), P(None, "rows", "ifg")),
        check_vma=False,
    )
```

```python
import functools

import numpy as np
import jax
import jax.numpy as jnp
from jax import lax
from jax.experimental import pallas as pl
from jax.experimental.pallas import tpu as pltpu
from jax.sharding import PartitionSpec as P

DATES = 96
SWEEPS = 4
HALO = SWEEPS
PI32 = float(np.float32(np.pi))
TWO_PI_HI = float(np.float32(2 * np.pi))
TWO_PI_LO = float(np.float32(2 * np.pi - np.float64(np.float32(2 * np.pi))))


def extended_2(block, sides, width):
    for axis, dim in sides:
        count = lax.axis_size(axis)
        forward = [(i, i + 1) for i in range(count - 1)]
        backward = [(target, source) for source, target in forward]
        low = lax.ppermute(
            lax.slice_in_dim(block, block.shape[dim] - width, None, axis=dim), axis, forward
        )
        high = lax.ppermute(lax.slice_in_dim(block, 0, width, axis=dim), axis, backward)
        block = jnp.concatenate([low, block, high], axis=dim)
    return block


def wrapped_diff(delta):
    above = (delta - TWO_PI_HI) - TWO_PI_LO
    below = (delta + TWO_PI_HI) + TWO_PI_LO
    return jnp.where(delta >= PI32, above, jnp.where(delta <= -PI32, below, delta))


def unwrap_kernel(rows_out, ph_ref, wt_ref, top_ref, bot_ref, o_ref, p_ref, q_ref, cur_ref):
    p_ref[pl.ds(0, HALO), :] = top_ref[0, 0]
    p_ref[pl.ds(HALO, rows_out), :] = ph_ref[0]
    p_ref[pl.ds(HALO + rows_out, HALO), :] = bot_ref[0, 0]
    q_ref[pl.ds(0, HALO), :] = top_ref[1, 0]
    q_ref[pl.ds(HALO, rows_out), :] = wt_ref[0].astype(jnp.float32)
    q_ref[pl.ds(HALO + rows_out, HALO), :] = bot_ref[1, 0]
    p = p_ref[...]
    q = q_ref[...]
    nr, nc = p.shape
    row = lax.broadcasted_iota(jnp.int32, (nr, nc), 0)
    col = lax.broadcasted_iota(jnp.int32, (nr, nc), 1)
    zero = jnp.zeros((nr, nc), jnp.float32)
    p_dn = pltpu.roll(p, nr - 1, 0)
    q_dn = pltpu.roll(q, nr - 1, 0)
    g_dn = wrapped_diff(p_dn - p)
    w_dn = jnp.where(row < nr - 1, q_dn * q, zero)
    p_rt = pltpu.roll(p, nc - 1, 1)
    q_rt = pltpu.roll(q, nc - 1, 1)
    g_rt = wrapped_diff(p_rt - p)
    w_rt = jnp.where(col < nc - 1, q_rt * q, zero)
    g_up = pltpu.roll(g_dn, 1, 0)
    w_up = pltpu.roll(w_dn, 1, 0)
    g_lt = pltpu.roll(g_rt, 1, 1)
    w_lt = pltpu.roll(w_rt, 1, 1)
    den = ((w_up + w_dn) + w_lt) + w_rt
    den = jnp.where(den > 0.0, den, 1.0)
    cur = zero
    for _ in range(SWEEPS):
        c_up = pltpu.roll(cur, 1, 0)
        c_dn = pltpu.roll(cur, nr - 1, 0)
        c_lt = pltpu.roll(cur, 1, 1)
        c_rt = pltpu.roll(cur, nc - 1, 1)
        num = w_up * (c_up + g_up)
        num = num + w_dn * (c_dn - g_dn)
        num = num + w_lt * (c_lt + g_lt)
        num = num + w_rt * (c_rt - g_rt)
        cur = num / den
    cur_ref[...] = cur
    half = rows_out // 2
    upper = cur_ref[pl.ds(HALO, half), :]
    lower = cur_ref[pl.ds(HALO + half, half), :]
    lane = lax.broadcasted_iota(jnp.int32, (half, nc), 1) % 128
    first = lane < 64
    even = jnp.where(first, upper, pltpu.roll(lower, 64, 1))
    odd = jnp.where(first, pltpu.roll(upper, nc - 64, 1), lower)
    for m in range(nc // 128):
        o_ref[2 * m, 0] = even[:, 128 * m : 128 * (m + 1)]
        o_ref[2 * m + 1, 0] = odd[:, 128 * m : 128 * (m + 1)]


def unwrap(phase, weights, top, bottom):
    n, rows_out, nc = phase.shape
    nr = rows_out + 2 * HALO
    halo_spec = pl.BlockSpec((2, 1, HALO, nc), lambda i: (0, i, 0, 0))
    return pl.pallas_call(
        functools.partial(unwrap_kernel, rows_out),
        grid=(n,),
        in_specs=[
            pl.BlockSpec((1, rows_out, nc), lambda i: (i, 0, 0)),
            pl.BlockSpec((1, rows_out, nc), lambda i: (i, 0, 0)),
            halo_spec,
            halo_spec,
        ],
        out_specs=pl.BlockSpec((nc // 64, 1, rows_out // 2, 128), lambda i: (0, i, 0, 0)),
        out_shape=jax.ShapeDtypeStruct((nc // 64, n, rows_out // 2, 128), jnp.float32),
        scratch_shapes=[pltpu.VMEM((nr, nc), jnp.float32)] * 3,
        cost_estimate=pl.CostEstimate(
            flops=120 * n * nr * nc, bytes_accessed=4 * n * nc * (2 * nr + rows_out), transcendentals=0
        ),
    )(phase, weights, top, bottom)


def binomial(padded, axis):
    length = padded.shape[axis] - 4

    def shifted(offset):
        return lax.slice_in_dim(padded, offset, offset + length, axis=axis)

    return (
        shifted(0) + 4.0 * shifted(1) + 6.0 * shifted(2) + 4.0 * shifted(3) + shifted(4)
    ) * 0.0625


def network_maps(network):
    date_ids = jnp.arange(DATES, dtype=jnp.int32)[None, :]
    full = (network[:, 1:2] == date_ids).astype(jnp.float32) - (network[:, 0:1] == date_ids).astype(
        jnp.float32
    )
    design = full[:, 1:]
    normal_matrix = jnp.dot(design.T, design, precision=lax.Precision.HIGHEST)
    factor = jnp.linalg.cholesky(normal_matrix)
    pseudo = jax.scipy.linalg.cho_solve((factor, True), design.T)
    return (design, pseudo)


def on_device(phase, weights, network):
    design, pseudo = network_maps(network)
    rows = phase.shape[1]
    count = lax.axis_size("rows")
    forward = [(i, i + 1) for i in range(count - 1)]
    backward = [(target, source) for source, target in forward]
    edge_low = jnp.stack([phase[:, rows - HALO :], weights[:, rows - HALO :].astype(jnp.float32)])
    edge_high = jnp.stack([phase[:, :HALO], weights[:, :HALO].astype(jnp.float32)])
    top = lax.ppermute(edge_low, "rows", forward)
    bottom = lax.ppermute(edge_high, "rows", backward)
    current = unwrap(phase, weights, top, bottom)
    received = lax.all_to_all(current, "ifg", split_axis=0, concat_axis=0, tiled=True)
    ifg = received.shape[0] * received.shape[1]
    block = received.reshape(ifg, rows // 2, 2, 64).transpose(0, 2, 1, 3).reshape(ifg, rows, 64)
    series_block = jnp.einsum("ei,irc->erc", pseudo, block, precision=lax.Precision.HIGHEST)
    residual = block - jnp.einsum(
        "ie,erc->irc", design, series_block, precision=lax.Precision.HIGHEST
    )
    padded = extended_2(residual, (("rows", 1), ("ifg", 2)), 2)
    filtered = binomial(binomial(padded, 1), 2)
    return (series_block, filtered.astype(jnp.bfloat16))


def solution(mesh):
    return jax.shard_map(
        on_device,
        mesh=mesh,
        in_specs=(P("ifg", "rows", None), P("ifg", "rows", None), P()),
        out_specs=(P(None, "rows", "ifg"), P(None, "rows", "ifg")),
        check_vma=False,
    )
```

```python
import functools

import numpy as np
import jax
import jax.numpy as jnp
from jax import lax
from jax.experimental import pallas as pl
from jax.experimental.pallas import tpu as pltpu
from jax.sharding import PartitionSpec as P

DATES = 96
SWEEPS = 4
HALO = SWEEPS
PI32 = float(np.float32(np.pi))
TWO_PI_HI = float(np.float32(2 * np.pi))
TWO_PI_LO = float(np.float32(2 * np.pi - np.float64(np.float32(2 * np.pi))))


def extended_2(block, sides, width):
    for axis, dim in sides:
        count = lax.axis_size(axis)
        forward = [(i, i + 1) for i in range(count - 1)]
        backward = [(target, source) for source, target in forward]
        low = lax.ppermute(
            lax.slice_in_dim(block, block.shape[dim] - width, None, axis=dim), axis, forward
        )
        high = lax.ppermute(lax.slice_in_dim(block, 0, width, axis=dim), axis, backward)
        block = jnp.concatenate([low, block, high], axis=dim)
    return block


def wrapped_diff(delta):
    above = (delta - TWO_PI_HI) - TWO_PI_LO
    below = (delta + TWO_PI_HI) + TWO_PI_LO
    return jnp.where(delta >= PI32, above, jnp.where(delta <= -PI32, below, delta))


def unwrap_kernel(rows_out, ph_ref, wt_ref, top_ref, bot_ref, o_ref, p_ref, q_ref, cur_ref):
    p_ref[pl.ds(0, HALO), :] = top_ref[0, 0]
    p_ref[pl.ds(HALO, rows_out), :] = ph_ref[0]
    p_ref[pl.ds(HALO + rows_out, HALO), :] = bot_ref[0, 0]
    q_ref[pl.ds(0, HALO), :] = top_ref[1, 0]
    q_ref[pl.ds(HALO, rows_out), :] = wt_ref[0].astype(jnp.float32)
    q_ref[pl.ds(HALO + rows_out, HALO), :] = bot_ref[1, 0]
    p = p_ref[...]
    q = q_ref[...]
    nr, nc = p.shape
    row = lax.broadcasted_iota(jnp.int32, (nr, nc), 0)
    col = lax.broadcasted_iota(jnp.int32, (nr, nc), 1)
    zero = jnp.zeros((nr, nc), jnp.float32)
    p_dn = pltpu.roll(p, nr - 1, 0)
    q_dn = pltpu.roll(q, nr - 1, 0)
    g_dn = wrapped_diff(p_dn - p)
    w_dn = jnp.where(row < nr - 1, q_dn * q, zero)
    p_rt = pltpu.roll(p, nc - 1, 1)
    q_rt = pltpu.roll(q, nc - 1, 1)
    g_rt = wrapped_diff(p_rt - p)
    w_rt = jnp.where(col < nc - 1, q_rt * q, zero)
    g_up = pltpu.roll(g_dn, 1, 0)
    w_up = pltpu.roll(w_dn, 1, 0)
    g_lt = pltpu.roll(g_rt, 1, 1)
    w_lt = pltpu.roll(w_rt, 1, 1)
    den = ((w_up + w_dn) + w_lt) + w_rt
    den = jnp.where(den > 0.0, den, 1.0)
    inv = 1.0 / den
    num = w_up * g_up
    num = num - w_dn * g_dn
    num = num + w_lt * g_lt
    num = num - w_rt * g_rt
    cur = num * inv
    for _ in range(SWEEPS - 1):
        c_up = pltpu.roll(cur, 1, 0)
        c_dn = pltpu.roll(cur, nr - 1, 0)
        c_lt = pltpu.roll(cur, 1, 1)
        c_rt = pltpu.roll(cur, nc - 1, 1)
        num = w_up * (c_up + g_up)
        num = num + w_dn * (c_dn - g_dn)
        num = num + w_lt * (c_lt + g_lt)
        num = num + w_rt * (c_rt - g_rt)
        cur = num * inv
    cur_ref[...] = cur
    half = rows_out // 2
    upper = cur_ref[pl.ds(HALO, half), :]
    lower = cur_ref[pl.ds(HALO + half, half), :]
    lane = lax.broadcasted_iota(jnp.int32, (half, nc), 1) % 128
    first = lane < 64
    even = jnp.where(first, upper, pltpu.roll(lower, 64, 1))
    odd = jnp.where(first, pltpu.roll(upper, nc - 64, 1), lower)
    for m in range(nc // 128):
        o_ref[2 * m, 0] = even[:, 128 * m : 128 * (m + 1)]
        o_ref[2 * m + 1, 0] = odd[:, 128 * m : 128 * (m + 1)]


def unwrap(phase, weights, top, bottom):
    n, rows_out, nc = phase.shape
    nr = rows_out + 2 * HALO
    halo_spec = pl.BlockSpec((2, 1, HALO, nc), lambda i: (0, i, 0, 0))
    return pl.pallas_call(
        functools.partial(unwrap_kernel, rows_out),
        grid=(n,),
        in_specs=[
            pl.BlockSpec((1, rows_out, nc), lambda i: (i, 0, 0)),
            pl.BlockSpec((1, rows_out, nc), lambda i: (i, 0, 0)),
            halo_spec,
            halo_spec,
        ],
        out_specs=pl.BlockSpec((nc // 64, 1, rows_out // 2, 128), lambda i: (0, i, 0, 0)),
        out_shape=jax.ShapeDtypeStruct((nc // 64, n, rows_out // 2, 128), jnp.float32),
        scratch_shapes=[pltpu.VMEM((nr, nc), jnp.float32)] * 3,
        cost_estimate=pl.CostEstimate(
            flops=120 * n * nr * nc, bytes_accessed=4 * n * nc * (2 * nr + rows_out), transcendentals=0
        ),
    )(phase, weights, top, bottom)


def binomial(padded, axis):
    length = padded.shape[axis] - 4

    def shifted(offset):
        return lax.slice_in_dim(padded, offset, offset + length, axis=axis)

    return (
        shifted(0) + 4.0 * shifted(1) + 6.0 * shifted(2) + 4.0 * shifted(3) + shifted(4)
    ) * 0.0625


def network_maps(network):
    date_ids = jnp.arange(DATES, dtype=jnp.int32)[None, :]
    full = (network[:, 1:2] == date_ids).astype(jnp.float32) - (network[:, 0:1] == date_ids).astype(
        jnp.float32
    )
    design = full[:, 1:]
    normal_matrix = jnp.dot(design.T, design, precision=lax.Precision.HIGHEST)
    factor = jnp.linalg.cholesky(normal_matrix)
    pseudo = jax.scipy.linalg.cho_solve((factor, True), design.T)
    return (design, pseudo)


def on_device(phase, weights, network):
    design, pseudo = network_maps(network)
    rows = phase.shape[1]
    count = lax.axis_size("rows")
    forward = [(i, i + 1) for i in range(count - 1)]
    backward = [(target, source) for source, target in forward]
    edge_low = jnp.stack([phase[:, rows - HALO :], weights[:, rows - HALO :].astype(jnp.float32)])
    edge_high = jnp.stack([phase[:, :HALO], weights[:, :HALO].astype(jnp.float32)])
    top = lax.ppermute(edge_low, "rows", forward)
    bottom = lax.ppermute(edge_high, "rows", backward)
    current = unwrap(phase, weights, top, bottom)
    received = lax.all_to_all(current, "ifg", split_axis=0, concat_axis=0, tiled=True)
    ifg = received.shape[0] * received.shape[1]
    block = received.reshape(ifg, rows // 2, 2, 64).transpose(0, 2, 1, 3).reshape(ifg, rows, 64)
    series_block = jnp.einsum("ei,irc->erc", pseudo, block, precision=lax.Precision.HIGHEST)
    residual = block - jnp.einsum(
        "ie,erc->irc", design, series_block, precision=lax.Precision.HIGHEST
    )
    padded = extended_2(residual, (("rows", 1), ("ifg", 2)), 2)
    filtered = binomial(binomial(padded, 1), 2)
    return (series_block, filtered.astype(jnp.bfloat16))


def solution(mesh):
    return jax.shard_map(
        on_device,
        mesh=mesh,
        in_specs=(P("ifg", "rows", None), P("ifg", "rows", None), P()),
        out_specs=(P(None, "rows", "ifg"), P(None, "rows", "ifg")),
        check_vma=False,
    )
```

```python
import functools

import numpy as np
import jax
import jax.numpy as jnp
from jax import lax
from jax.experimental import pallas as pl
from jax.experimental.pallas import tpu as pltpu
from jax.sharding import PartitionSpec as P

DATES = 96
SWEEPS = 4
HALO = SWEEPS
PI32 = float(np.float32(np.pi))
TWO_PI_HI = float(np.float32(2 * np.pi))
TWO_PI_LO = float(np.float32(2 * np.pi - np.float64(np.float32(2 * np.pi))))


def extended_2(block, sides, width):
    for axis, dim in sides:
        count = lax.axis_size(axis)
        forward = [(i, i + 1) for i in range(count - 1)]
        backward = [(target, source) for source, target in forward]
        low = lax.ppermute(
            lax.slice_in_dim(block, block.shape[dim] - width, None, axis=dim), axis, forward
        )
        high = lax.ppermute(lax.slice_in_dim(block, 0, width, axis=dim), axis, backward)
        block = jnp.concatenate([low, block, high], axis=dim)
    return block


def wrapped_diff(delta):
    above = (delta - TWO_PI_HI) - TWO_PI_LO
    below = (delta + TWO_PI_HI) + TWO_PI_LO
    return jnp.where(delta >= PI32, above, jnp.where(delta <= -PI32, below, delta))


def unwrap_kernel(rows_out, ph_ref, wt_ref, top_ref, bot_ref, o_ref, p_ref, q_ref, cur_ref):
    p_ref[pl.ds(0, HALO), :] = top_ref[0, 0]
    p_ref[pl.ds(HALO, rows_out), :] = ph_ref[0]
    p_ref[pl.ds(HALO + rows_out, HALO), :] = bot_ref[0, 0]
    q_ref[pl.ds(0, HALO), :] = top_ref[1, 0]
    q_ref[pl.ds(HALO, rows_out), :] = wt_ref[0].astype(jnp.float32)
    q_ref[pl.ds(HALO + rows_out, HALO), :] = bot_ref[1, 0]
    p = p_ref[...]
    q = q_ref[...]
    nr, nc = p.shape
    row = lax.broadcasted_iota(jnp.int32, (nr, nc), 0)
    col = lax.broadcasted_iota(jnp.int32, (nr, nc), 1)
    zero = jnp.zeros((nr, nc), jnp.float32)
    p_dn = pltpu.roll(p, nr - 1, 0)
    q_dn = pltpu.roll(q, nr - 1, 0)
    g_dn = wrapped_diff(p_dn - p)
    w_dn = jnp.where(row < nr - 1, q_dn * q, zero)
    p_rt = pltpu.roll(p, nc - 1, 1)
    q_rt = pltpu.roll(q, nc - 1, 1)
    g_rt = wrapped_diff(p_rt - p)
    w_rt = jnp.where(col < nc - 1, q_rt * q, zero)
    g_up = pltpu.roll(g_dn, 1, 0)
    w_up = pltpu.roll(w_dn, 1, 0)
    g_lt = pltpu.roll(g_rt, 1, 1)
    w_lt = pltpu.roll(w_rt, 1, 1)
    den = ((w_up + w_dn) + w_lt) + w_rt
    den = jnp.where(den > 0.0, den, 1.0)
    inv = 1.0 / den
    num = w_up * g_up
    num = num - w_dn * g_dn
    num = num + w_lt * g_lt
    num = num - w_rt * g_rt
    const = num * inv
    a_up, a_dn, a_lt, a_rt = w_up * inv, w_dn * inv, w_lt * inv, w_rt * inv
    cur = const
    for _ in range(SWEEPS - 1):
        nxt = const + a_up * pltpu.roll(cur, 1, 0)
        nxt = nxt + a_dn * pltpu.roll(cur, nr - 1, 0)
        nxt = nxt + a_lt * pltpu.roll(cur, 1, 1)
        nxt = nxt + a_rt * pltpu.roll(cur, nc - 1, 1)
        cur = nxt
    cur_ref[...] = cur
    half = rows_out // 2
    upper = cur_ref[pl.ds(HALO, half), :]
    lower = cur_ref[pl.ds(HALO + half, half), :]
    lane = lax.broadcasted_iota(jnp.int32, (half, nc), 1) % 128
    first = lane < 64
    even = jnp.where(first, upper, pltpu.roll(lower, 64, 1))
    odd = jnp.where(first, pltpu.roll(upper, nc - 64, 1), lower)
    for m in range(nc // 128):
        o_ref[2 * m, 0] = even[:, 128 * m : 128 * (m + 1)]
        o_ref[2 * m + 1, 0] = odd[:, 128 * m : 128 * (m + 1)]


def unwrap(phase, weights, top, bottom):
    n, rows_out, nc = phase.shape
    nr = rows_out + 2 * HALO
    halo_spec = pl.BlockSpec((2, 1, HALO, nc), lambda i: (0, i, 0, 0))
    return pl.pallas_call(
        functools.partial(unwrap_kernel, rows_out),
        grid=(n,),
        in_specs=[
            pl.BlockSpec((1, rows_out, nc), lambda i: (i, 0, 0)),
            pl.BlockSpec((1, rows_out, nc), lambda i: (i, 0, 0)),
            halo_spec,
            halo_spec,
        ],
        out_specs=pl.BlockSpec((nc // 64, 1, rows_out // 2, 128), lambda i: (0, i, 0, 0)),
        out_shape=jax.ShapeDtypeStruct((nc // 64, n, rows_out // 2, 128), jnp.float32),
        scratch_shapes=[pltpu.VMEM((nr, nc), jnp.float32)] * 3,
        cost_estimate=pl.CostEstimate(
            flops=120 * n * nr * nc, bytes_accessed=4 * n * nc * (2 * nr + rows_out), transcendentals=0
        ),
    )(phase, weights, top, bottom)


def binomial(padded, axis):
    length = padded.shape[axis] - 4

    def shifted(offset):
        return lax.slice_in_dim(padded, offset, offset + length, axis=axis)

    return (
        shifted(0) + 4.0 * shifted(1) + 6.0 * shifted(2) + 4.0 * shifted(3) + shifted(4)
    ) * 0.0625


def network_maps(network):
    date_ids = jnp.arange(DATES, dtype=jnp.int32)[None, :]
    full = (network[:, 1:2] == date_ids).astype(jnp.float32) - (network[:, 0:1] == date_ids).astype(
        jnp.float32
    )
    design = full[:, 1:]
    normal_matrix = jnp.dot(design.T, design, precision=lax.Precision.HIGHEST)
    factor = jnp.linalg.cholesky(normal_matrix)
    pseudo = jax.scipy.linalg.cho_solve((factor, True), design.T)
    return (design, pseudo)


def on_device(phase, weights, network):
    design, pseudo = network_maps(network)
    rows = phase.shape[1]
    count = lax.axis_size("rows")
    forward = [(i, i + 1) for i in range(count - 1)]
    backward = [(target, source) for source, target in forward]
    edge_low = jnp.stack([phase[:, rows - HALO :], weights[:, rows - HALO :].astype(jnp.float32)])
    edge_high = jnp.stack([phase[:, :HALO], weights[:, :HALO].astype(jnp.float32)])
    top = lax.ppermute(edge_low, "rows", forward)
    bottom = lax.ppermute(edge_high, "rows", backward)
    current = unwrap(phase, weights, top, bottom)
    received = lax.all_to_all(current, "ifg", split_axis=0, concat_axis=0, tiled=True)
    ifg = received.shape[0] * received.shape[1]
    block = received.reshape(ifg, rows // 2, 2, 64).transpose(0, 2, 1, 3).reshape(ifg, rows, 64)
    series_block = jnp.einsum("ei,irc->erc", pseudo, block, precision=lax.Precision.HIGHEST)
    residual = block - jnp.einsum(
        "ie,erc->irc", design, series_block, precision=lax.Precision.HIGHEST
    )
    padded = extended_2(residual, (("rows", 1), ("ifg", 2)), 2)
    filtered = binomial(binomial(padded, 1), 2)
    return (series_block, filtered.astype(jnp.bfloat16))


def solution(mesh):
    return jax.shard_map(
        on_device,
        mesh=mesh,
        in_specs=(P("ifg", "rows", None), P("ifg", "rows", None), P()),
        out_specs=(P(None, "rows", "ifg"), P(None, "rows", "ifg")),
        check_vma=False,
    )
```

```python
import functools

import numpy as np
import jax
import jax.numpy as jnp
from jax import lax
from jax.experimental import pallas as pl
from jax.experimental.pallas import tpu as pltpu
from jax.sharding import PartitionSpec as P

DATES = 96
SWEEPS = 4
FILTER_HALO = 2
HALO = 8
PI32 = float(np.float32(np.pi))
TWO_PI_HI = float(np.float32(2 * np.pi))
TWO_PI_LO = float(np.float32(2 * np.pi - np.float64(np.float32(2 * np.pi))))


def extended_2(block, sides, width):
    for axis, dim in sides:
        count = lax.axis_size(axis)
        forward = [(i, i + 1) for i in range(count - 1)]
        backward = [(target, source) for source, target in forward]
        low = lax.ppermute(
            lax.slice_in_dim(block, block.shape[dim] - width, None, axis=dim), axis, forward
        )
        high = lax.ppermute(lax.slice_in_dim(block, 0, width, axis=dim), axis, backward)
        block = jnp.concatenate([low, block, high], axis=dim)
    return block


def wrapped_diff(delta):
    above = (delta - TWO_PI_HI) - TWO_PI_LO
    below = (delta + TWO_PI_HI) + TWO_PI_LO
    return jnp.where(delta >= PI32, above, jnp.where(delta <= -PI32, below, delta))


def unwrap_kernel(rows_out, ph_ref, wt_ref, top_ref, bot_ref, o_ref, p_ref, q_ref, cur_ref):
    p_ref[pl.ds(0, HALO), :] = top_ref[0, 0]
    p_ref[pl.ds(HALO, rows_out), :] = ph_ref[0]
    p_ref[pl.ds(HALO + rows_out, HALO), :] = bot_ref[0, 0]
    q_ref[pl.ds(0, HALO), :] = top_ref[1, 0]
    q_ref[pl.ds(HALO, rows_out), :] = wt_ref[0].astype(jnp.float32)
    q_ref[pl.ds(HALO + rows_out, HALO), :] = bot_ref[1, 0]
    p = p_ref[...]
    q = q_ref[...]
    nr, nc = p.shape
    row = lax.broadcasted_iota(jnp.int32, (nr, nc), 0)
    col = lax.broadcasted_iota(jnp.int32, (nr, nc), 1)
    zero = jnp.zeros((nr, nc), jnp.float32)
    p_dn = pltpu.roll(p, nr - 1, 0)
    q_dn = pltpu.roll(q, nr - 1, 0)
    g_dn = wrapped_diff(p_dn - p)
    w_dn = jnp.where(row < nr - 1, q_dn * q, zero)
    p_rt = pltpu.roll(p, nc - 1, 1)
    q_rt = pltpu.roll(q, nc - 1, 1)
    g_rt = wrapped_diff(p_rt - p)
    w_rt = jnp.where(col < nc - 1, q_rt * q, zero)
    g_up = pltpu.roll(g_dn, 1, 0)
    w_up = pltpu.roll(w_dn, 1, 0)
    g_lt = pltpu.roll(g_rt, 1, 1)
    w_lt = pltpu.roll(w_rt, 1, 1)
    den = ((w_up + w_dn) + w_lt) + w_rt
    den = jnp.where(den > 0.0, den, 1.0)
    inv = 1.0 / den
    num = w_up * g_up
    num = num - w_dn * g_dn
    num = num + w_lt * g_lt
    num = num - w_rt * g_rt
    const = num * inv
    a_up, a_dn, a_lt, a_rt = w_up * inv, w_dn * inv, w_lt * inv, w_rt * inv
    cur = const
    for _ in range(SWEEPS - 1):
        nxt = const + a_up * pltpu.roll(cur, 1, 0)
        nxt = nxt + a_dn * pltpu.roll(cur, nr - 1, 0)
        nxt = nxt + a_lt * pltpu.roll(cur, 1, 1)
        nxt = nxt + a_rt * pltpu.roll(cur, nc - 1, 1)
        cur = nxt
    cur_ref[...] = cur
    half = rows_out // 2 + FILTER_HALO
    upper = cur_ref[pl.ds(HALO - FILTER_HALO, half), :]
    lower = cur_ref[pl.ds(HALO - FILTER_HALO + half, half), :]
    lane = lax.broadcasted_iota(jnp.int32, (half, nc), 1) % 128
    first = lane < 64
    even = jnp.where(first, upper, pltpu.roll(lower, 64, 1))
    odd = jnp.where(first, pltpu.roll(upper, nc - 64, 1), lower)
    for m in range(nc // 128):
        o_ref[2 * m, 0] = even[:, 128 * m : 128 * (m + 1)]
        o_ref[2 * m + 1, 0] = odd[:, 128 * m : 128 * (m + 1)]


def unwrap(phase, weights, top, bottom):
    n, rows_out, nc = phase.shape
    nr = rows_out + 2 * HALO
    half = rows_out // 2 + FILTER_HALO
    halo_spec = pl.BlockSpec((2, 1, HALO, nc), lambda i: (0, i, 0, 0))
    return pl.pallas_call(
        functools.partial(unwrap_kernel, rows_out),
        grid=(n,),
        in_specs=[
            pl.BlockSpec((1, rows_out, nc), lambda i: (i, 0, 0)),
            pl.BlockSpec((1, rows_out, nc), lambda i: (i, 0, 0)),
            halo_spec,
            halo_spec,
        ],
        out_specs=pl.BlockSpec((nc // 64, 1, half, 128), lambda i: (0, i, 0, 0)),
        out_shape=jax.ShapeDtypeStruct((nc // 64, n, half, 128), jnp.float32),
        scratch_shapes=[pltpu.VMEM((nr, nc), jnp.float32)] * 3,
        cost_estimate=pl.CostEstimate(
            flops=120 * n * nr * nc, bytes_accessed=4 * n * nc * (2 * nr + rows_out), transcendentals=0
        ),
    )(phase, weights, top, bottom)


def binomial(padded, axis):
    length = padded.shape[axis] - 4

    def shifted(offset):
        return lax.slice_in_dim(padded, offset, offset + length, axis=axis)

    return (
        shifted(0) + 4.0 * shifted(1) + 6.0 * shifted(2) + 4.0 * shifted(3) + shifted(4)
    ) * 0.0625


def network_maps(network):
    date_ids = jnp.arange(DATES, dtype=jnp.int32)[None, :]
    full = (network[:, 1:2] == date_ids).astype(jnp.float32) - (network[:, 0:1] == date_ids).astype(
        jnp.float32
    )
    design = full[:, 1:]
    normal_matrix = jnp.dot(design.T, design, precision=lax.Precision.HIGHEST)
    factor = jnp.linalg.cholesky(normal_matrix)
    pseudo = jax.scipy.linalg.cho_solve((factor, True), design.T)
    return (design, pseudo)


def on_device(phase, weights, network):
    design, pseudo = network_maps(network)
    rows = phase.shape[1]
    count = lax.axis_size("rows")
    forward = [(i, i + 1) for i in range(count - 1)]
    backward = [(target, source) for source, target in forward]
    edge_low = jnp.stack([phase[:, rows - HALO :], weights[:, rows - HALO :].astype(jnp.float32)])
    edge_high = jnp.stack([phase[:, :HALO], weights[:, :HALO].astype(jnp.float32)])
    top = lax.ppermute(edge_low, "rows", forward)
    bottom = lax.ppermute(edge_high, "rows", backward)
    current = unwrap(phase, weights, top, bottom)
    received = lax.all_to_all(current, "ifg", split_axis=0, concat_axis=0, tiled=True)
    ifg = received.shape[0] * received.shape[1]
    tall = rows + 2 * FILTER_HALO
    block = received.reshape(ifg, tall // 2, 2, 64).transpose(0, 2, 1, 3).reshape(ifg, tall, 64)
    series_block = jnp.einsum("ei,irc->erc", pseudo, block, precision=lax.Precision.HIGHEST)
    residual = block - jnp.einsum(
        "ie,erc->irc", design, series_block, precision=lax.Precision.HIGHEST
    )
    padded = extended_2(residual, (("ifg", 2),), FILTER_HALO)
    filtered = binomial(binomial(padded, 1), 2)
    series_block = series_block[:, FILTER_HALO : FILTER_HALO + rows]
    return (series_block, filtered.astype(jnp.bfloat16))


def solution(mesh):
    return jax.shard_map(
        on_device,
        mesh=mesh,
        in_specs=(P("ifg", "rows", None), P("ifg", "rows", None), P()),
        out_specs=(P(None, "rows", "ifg"), P(None, "rows", "ifg")),
        check_vma=False,
    )
```

```python
import functools

import numpy as np
import jax
import jax.numpy as jnp
from jax import lax
from jax.experimental import pallas as pl
from jax.experimental.pallas import tpu as pltpu
from jax.sharding import PartitionSpec as P

DATES = 96
SWEEPS = 4
HALO = SWEEPS
PI32 = float(np.float32(np.pi))
TWO_PI_HI = float(np.float32(2 * np.pi))
TWO_PI_LO = float(np.float32(2 * np.pi - np.float64(np.float32(2 * np.pi))))


def extended_2(block, sides, width):
    for axis, dim in sides:
        count = lax.axis_size(axis)
        forward = [(i, i + 1) for i in range(count - 1)]
        backward = [(target, source) for source, target in forward]
        low = lax.ppermute(
            lax.slice_in_dim(block, block.shape[dim] - width, None, axis=dim), axis, forward
        )
        high = lax.ppermute(lax.slice_in_dim(block, 0, width, axis=dim), axis, backward)
        block = jnp.concatenate([low, block, high], axis=dim)
    return block


def wrapped_diff(delta):
    above = (delta - TWO_PI_HI) - TWO_PI_LO
    below = (delta + TWO_PI_HI) + TWO_PI_LO
    return jnp.where(delta >= PI32, above, jnp.where(delta <= -PI32, below, delta))


def unwrap_kernel(rows_out, ph_ref, wt_ref, top_ref, bot_ref, o_ref, p_ref, q_ref, cur_ref):
    for b in range(ph_ref.shape[0]):
        p_ref[pl.ds(0, HALO), :] = top_ref[0, b]
        p_ref[pl.ds(HALO, rows_out), :] = ph_ref[b]
        p_ref[pl.ds(HALO + rows_out, HALO), :] = bot_ref[0, b]
        q_ref[pl.ds(0, HALO), :] = top_ref[1, b]
        q_ref[pl.ds(HALO, rows_out), :] = wt_ref[b].astype(jnp.float32)
        q_ref[pl.ds(HALO + rows_out, HALO), :] = bot_ref[1, b]
        p = p_ref[...]
        q = q_ref[...]
        nr, nc = p.shape
        row = lax.broadcasted_iota(jnp.int32, (nr, nc), 0)
        col = lax.broadcasted_iota(jnp.int32, (nr, nc), 1)
        zero = jnp.zeros((nr, nc), jnp.float32)
        p_dn = pltpu.roll(p, nr - 1, 0)
        q_dn = pltpu.roll(q, nr - 1, 0)
        g_dn = wrapped_diff(p_dn - p)
        w_dn = jnp.where(row < nr - 1, q_dn * q, zero)
        p_rt = pltpu.roll(p, nc - 1, 1)
        q_rt = pltpu.roll(q, nc - 1, 1)
        g_rt = wrapped_diff(p_rt - p)
        w_rt = jnp.where(col < nc - 1, q_rt * q, zero)
        g_up = pltpu.roll(g_dn, 1, 0)
        w_up = pltpu.roll(w_dn, 1, 0)
        g_lt = pltpu.roll(g_rt, 1, 1)
        w_lt = pltpu.roll(w_rt, 1, 1)
        den = ((w_up + w_dn) + w_lt) + w_rt
        den = jnp.where(den > 0.0, den, 1.0)
        inv = 1.0 / den
        num = w_up * g_up
        num = num - w_dn * g_dn
        num = num + w_lt * g_lt
        num = num - w_rt * g_rt
        const = num * inv
        a_up, a_dn, a_lt, a_rt = w_up * inv, w_dn * inv, w_lt * inv, w_rt * inv
        cur = const
        for _ in range(SWEEPS - 1):
            nxt = const + a_up * pltpu.roll(cur, 1, 0)
            nxt = nxt + a_dn * pltpu.roll(cur, nr - 1, 0)
            nxt = nxt + a_lt * pltpu.roll(cur, 1, 1)
            nxt = nxt + a_rt * pltpu.roll(cur, nc - 1, 1)
            cur = nxt
        cur_ref[...] = cur
        half = rows_out // 2
        upper = cur_ref[pl.ds(HALO, half), :]
        lower = cur_ref[pl.ds(HALO + half, half), :]
        lane = lax.broadcasted_iota(jnp.int32, (half, nc), 1) % 128
        first = lane < 64
        even = jnp.where(first, upper, pltpu.roll(lower, 64, 1))
        odd = jnp.where(first, pltpu.roll(upper, nc - 64, 1), lower)
        for m in range(nc // 128):
            o_ref[2 * m, b] = even[:, 128 * m : 128 * (m + 1)]
            o_ref[2 * m + 1, b] = odd[:, 128 * m : 128 * (m + 1)]


def unwrap(phase, weights, top, bottom):
    n, rows_out, nc = phase.shape
    nr = rows_out + 2 * HALO
    per = 2
    halo_spec = pl.BlockSpec((2, per, HALO, nc), lambda i: (0, i, 0, 0))
    return pl.pallas_call(
        functools.partial(unwrap_kernel, rows_out),
        grid=(n // per,),
        in_specs=[
            pl.BlockSpec((per, rows_out, nc), lambda i: (i, 0, 0)),
            pl.BlockSpec((per, rows_out, nc), lambda i: (i, 0, 0)),
            halo_spec,
            halo_spec,
        ],
        out_specs=pl.BlockSpec((nc // 64, per, rows_out // 2, 128), lambda i: (0, i, 0, 0)),
        out_shape=jax.ShapeDtypeStruct((nc // 64, n, rows_out // 2, 128), jnp.float32),
        scratch_shapes=[pltpu.VMEM((nr, nc), jnp.float32)] * 3,
        cost_estimate=pl.CostEstimate(
            flops=120 * n * nr * nc, bytes_accessed=4 * n * nc * (2 * nr + rows_out), transcendentals=0
        ),
    )(phase, weights, top, bottom)


def binomial(padded, axis):
    length = padded.shape[axis] - 4

    def shifted(offset):
        return lax.slice_in_dim(padded, offset, offset + length, axis=axis)

    return (
        shifted(0) + 4.0 * shifted(1) + 6.0 * shifted(2) + 4.0 * shifted(3) + shifted(4)
    ) * 0.0625


def network_maps(network):
    date_ids = jnp.arange(DATES, dtype=jnp.int32)[None, :]
    full = (network[:, 1:2] == date_ids).astype(jnp.float32) - (network[:, 0:1] == date_ids).astype(
        jnp.float32
    )
    design = full[:, 1:]
    normal_matrix = jnp.dot(design.T, design, precision=lax.Precision.HIGHEST)
    factor = jnp.linalg.cholesky(normal_matrix)
    pseudo = jax.scipy.linalg.cho_solve((factor, True), design.T)
    return (design, pseudo)


def on_device(phase, weights, network):
    design, pseudo = network_maps(network)
    rows = phase.shape[1]
    count = lax.axis_size("rows")
    forward = [(i, i + 1) for i in range(count - 1)]
    backward = [(target, source) for source, target in forward]
    edge_low = jnp.stack([phase[:, rows - HALO :], weights[:, rows - HALO :].astype(jnp.float32)])
    edge_high = jnp.stack([phase[:, :HALO], weights[:, :HALO].astype(jnp.float32)])
    top = lax.ppermute(edge_low, "rows", forward)
    bottom = lax.ppermute(edge_high, "rows", backward)
    current = unwrap(phase, weights, top, bottom)
    received = lax.all_to_all(current, "ifg", split_axis=0, concat_axis=0, tiled=True)
    ifg = received.shape[0] * received.shape[1]
    block = received.reshape(ifg, rows // 2, 2, 64).transpose(0, 2, 1, 3).reshape(ifg, rows, 64)
    series_block = jnp.einsum("ei,irc->erc", pseudo, block, precision=lax.Precision.HIGHEST)
    residual = block - jnp.einsum(
        "ie,erc->irc", design, series_block, precision=lax.Precision.HIGHEST
    )
    padded = extended_2(residual, (("rows", 1), ("ifg", 2)), 2)
    filtered = binomial(binomial(padded, 1), 2)
    return (series_block, filtered.astype(jnp.bfloat16))


def solution(mesh):
    return jax.shard_map(
        on_device,
        mesh=mesh,
        in_specs=(P("ifg", "rows", None), P("ifg", "rows", None), P()),
        out_specs=(P(None, "rows", "ifg"), P(None, "rows", "ifg")),
        check_vma=False,
    )
```

```python
import functools

import numpy as np
import jax
import jax.numpy as jnp
from jax import lax
from jax.experimental import pallas as pl
from jax.experimental.pallas import tpu as pltpu
from jax.sharding import PartitionSpec as P

DATES = 96
SWEEPS = 4
HALO = SWEEPS
PI32 = float(np.float32(np.pi))
TWO_PI_HI = float(np.float32(2 * np.pi))
TWO_PI_LO = float(np.float32(2 * np.pi - np.float64(np.float32(2 * np.pi))))


def extended_2(block, sides, width):
    for axis, dim in sides:
        count = lax.axis_size(axis)
        forward = [(i, i + 1) for i in range(count - 1)]
        backward = [(target, source) for source, target in forward]
        low = lax.ppermute(
            lax.slice_in_dim(block, block.shape[dim] - width, None, axis=dim), axis, forward
        )
        high = lax.ppermute(lax.slice_in_dim(block, 0, width, axis=dim), axis, backward)
        block = jnp.concatenate([low, block, high], axis=dim)
    return block


def wrapped_diff(delta):
    above = (delta - TWO_PI_HI) - TWO_PI_LO
    below = (delta + TWO_PI_HI) + TWO_PI_LO
    return jnp.where(delta >= PI32, above, jnp.where(delta <= -PI32, below, delta))


def unwrap_kernel(rows_out, ph_ref, wt_ref, top_ref, bot_ref, o_ref, p_ref, q_ref, cur_ref):
    for b in range(ph_ref.shape[0]):
        p_ref[pl.ds(0, HALO), :] = top_ref[0, b]
        p_ref[pl.ds(HALO, rows_out), :] = ph_ref[b]
        p_ref[pl.ds(HALO + rows_out, HALO), :] = bot_ref[0, b]
        q_ref[pl.ds(0, HALO), :] = top_ref[1, b]
        q_ref[pl.ds(HALO, rows_out), :] = wt_ref[b].astype(jnp.float32)
        q_ref[pl.ds(HALO + rows_out, HALO), :] = bot_ref[1, b]
        p = p_ref[...]
        q = q_ref[...]
        nr, nc = p.shape
        row = lax.broadcasted_iota(jnp.int32, (nr, nc), 0)
        col = lax.broadcasted_iota(jnp.int32, (nr, nc), 1)
        zero = jnp.zeros((nr, nc), jnp.float32)
        p_dn = pltpu.roll(p, nr - 1, 0)
        q_dn = pltpu.roll(q, nr - 1, 0)
        g_dn = wrapped_diff(p_dn - p)
        w_dn = jnp.where(row < nr - 1, q_dn * q, zero)
        p_rt = pltpu.roll(p, nc - 1, 1)
        q_rt = pltpu.roll(q, nc - 1, 1)
        g_rt = wrapped_diff(p_rt - p)
        w_rt = jnp.where(col < nc - 1, q_rt * q, zero)
        g_up = pltpu.roll(g_dn, 1, 0)
        w_up = pltpu.roll(w_dn, 1, 0)
        g_lt = pltpu.roll(g_rt, 1, 1)
        w_lt = pltpu.roll(w_rt, 1, 1)
        den = ((w_up + w_dn) + w_lt) + w_rt
        den = jnp.where(den > 0.0, den, 1.0)
        inv = 1.0 / den
        num = w_up * g_up
        num = num - w_dn * g_dn
        num = num + w_lt * g_lt
        num = num - w_rt * g_rt
        const = num * inv
        a_up, a_dn, a_lt, a_rt = w_up * inv, w_dn * inv, w_lt * inv, w_rt * inv
        cur = const
        for _ in range(SWEEPS - 1):
            nxt = const + a_up * pltpu.roll(cur, 1, 0)
            nxt = nxt + a_dn * pltpu.roll(cur, nr - 1, 0)
            nxt = nxt + a_lt * pltpu.roll(cur, 1, 1)
            nxt = nxt + a_rt * pltpu.roll(cur, nc - 1, 1)
            cur = nxt
        cur_ref[...] = cur
        half = rows_out // 2
        upper = cur_ref[pl.ds(HALO, half), :]
        lower = cur_ref[pl.ds(HALO + half, half), :]
        lane = lax.broadcasted_iota(jnp.int32, (half, nc), 1) % 128
        first = lane < 64
        even = jnp.where(first, upper, pltpu.roll(lower, 64, 1))
        odd = jnp.where(first, pltpu.roll(upper, nc - 64, 1), lower)
        for m in range(nc // 128):
            o_ref[2 * m, b] = even[:, 128 * m : 128 * (m + 1)]
            o_ref[2 * m + 1, b] = odd[:, 128 * m : 128 * (m + 1)]


def unwrap(phase, weights, top, bottom):
    n, rows_out, nc = phase.shape
    nr = rows_out + 2 * HALO
    per = 2
    halo_spec = pl.BlockSpec((2, per, HALO, nc), lambda i: (0, i, 0, 0))
    return pl.pallas_call(
        functools.partial(unwrap_kernel, rows_out),
        grid=(n // per,),
        in_specs=[
            pl.BlockSpec((per, rows_out, nc), lambda i: (i, 0, 0)),
            pl.BlockSpec((per, rows_out, nc), lambda i: (i, 0, 0)),
            halo_spec,
            halo_spec,
        ],
        out_specs=pl.BlockSpec((nc // 64, per, rows_out // 2, 128), lambda i: (0, i, 0, 0)),
        out_shape=jax.ShapeDtypeStruct((nc // 64, n, rows_out // 2, 128), jnp.float32),
        scratch_shapes=[pltpu.VMEM((nr, nc), jnp.float32)] * 3,
        cost_estimate=pl.CostEstimate(
            flops=120 * n * nr * nc, bytes_accessed=4 * n * nc * (2 * nr + rows_out), transcendentals=0
        ),
    )(phase, weights, top, bottom)


def invert_kernel(rows, x_ref, pseudo_ref, design_ref, s_ref, r_ref):
    ifg = pseudo_ref.shape[1]
    pseudo = pseudo_ref[...]
    design = design_ref[...]
    for k in range(rows):
        x = x_ref[pl.ds(k, ifg, stride=rows), :]
        series = jnp.dot(pseudo, x, precision=lax.Precision.HIGHEST, preferred_element_type=jnp.float32)
        fit = jnp.dot(design, series, precision=lax.Precision.HIGHEST, preferred_element_type=jnp.float32)
        res_t = (x - fit).T
        ser_t = series.T
        r_ref[pl.ds(k * 64, 64), :] = res_t[:64]
        r_ref[pl.ds((k + rows) * 64, 64), :] = res_t[64:]
        s_ref[pl.ds(k * 64, 64), :] = ser_t[:64]
        s_ref[pl.ds((k + rows) * 64, 64), :] = ser_t[64:]


def invert(packed, pseudo, design, rows):
    ifg = pseudo.shape[1]
    epochs = pseudo.shape[0]
    wide = epochs + (-epochs) % 8
    pseudo = jnp.pad(pseudo, ((0, wide - epochs), (0, 0)))
    design = jnp.pad(design, ((0, 0), (0, wide - epochs)))
    whole = pl.BlockSpec(memory_space=pltpu.VMEM)
    series_t, residual_t = pl.pallas_call(
        functools.partial(invert_kernel, rows),
        in_specs=[whole, whole, whole],
        out_specs=(whole, whole),
        out_shape=(
            jax.ShapeDtypeStruct((2 * rows * 64, wide), jnp.float32),
            jax.ShapeDtypeStruct((2 * rows * 64, ifg), jnp.float32),
        ),
        cost_estimate=pl.CostEstimate(
            flops=4 * 6 * wide * ifg * rows * 128,
            bytes_accessed=4 * 128 * rows * (2 * ifg + wide),
            transcendentals=0,
        ),
    )(packed, pseudo, design)
    return series_t[:, :epochs], residual_t


def binomial(padded, axis):
    length = padded.shape[axis] - 4

    def shifted(offset):
        return lax.slice_in_dim(padded, offset, offset + length, axis=axis)

    return (
        shifted(0) + 4.0 * shifted(1) + 6.0 * shifted(2) + 4.0 * shifted(3) + shifted(4)
    ) * 0.0625


def network_maps(network):
    date_ids = jnp.arange(DATES, dtype=jnp.int32)[None, :]
    full = (network[:, 1:2] == date_ids).astype(jnp.float32) - (network[:, 0:1] == date_ids).astype(
        jnp.float32
    )
    design = full[:, 1:]
    normal_matrix = jnp.dot(design.T, design, precision=lax.Precision.HIGHEST)
    factor = jnp.linalg.cholesky(normal_matrix)
    pseudo = jax.scipy.linalg.cho_solve((factor, True), design.T)
    return (design, pseudo)


def on_device(phase, weights, network):
    design, pseudo = network_maps(network)
    rows = phase.shape[1]
    count = lax.axis_size("rows")
    forward = [(i, i + 1) for i in range(count - 1)]
    backward = [(target, source) for source, target in forward]
    edge_low = jnp.stack([phase[:, rows - HALO :], weights[:, rows - HALO :].astype(jnp.float32)])
    edge_high = jnp.stack([phase[:, :HALO], weights[:, :HALO].astype(jnp.float32)])
    top = lax.ppermute(edge_low, "rows", forward)
    bottom = lax.ppermute(edge_high, "rows", backward)
    current = unwrap(phase, weights, top, bottom)
    received = lax.all_to_all(current, "ifg", split_axis=0, concat_axis=0, tiled=True)
    ifg = received.shape[0] * received.shape[1]
    half = rows // 2
    series_t, residual_t = invert(received.reshape(ifg * half, 128), pseudo, design, half)

    def unpack(x):
        return x.reshape(rows, 64, x.shape[1]).transpose(2, 0, 1)

    series_block = unpack(series_t)
    residual = unpack(residual_t)
    padded = extended_2(residual, (("rows", 1), ("ifg", 2)), 2)
    filtered = binomial(binomial(padded, 1), 2)
    return (series_block, filtered.astype(jnp.bfloat16))


def solution(mesh):
    return jax.shard_map(
        on_device,
        mesh=mesh,
        in_specs=(P("ifg", "rows", None), P("ifg", "rows", None), P()),
        out_specs=(P(None, "rows", "ifg"), P(None, "rows", "ifg")),
        check_vma=False,
    )
```

```python
import functools

import numpy as np
import jax
import jax.numpy as jnp
from jax import lax
from jax.experimental import pallas as pl
from jax.experimental.pallas import tpu as pltpu
from jax.sharding import PartitionSpec as P

DATES = 96
SWEEPS = 4
HALO = SWEEPS
PI32 = float(np.float32(np.pi))
TWO_PI_HI = float(np.float32(2 * np.pi))
TWO_PI_LO = float(np.float32(2 * np.pi - np.float64(np.float32(2 * np.pi))))


def extended_2(block, sides, width):
    for axis, dim in sides:
        count = lax.axis_size(axis)
        forward = [(i, i + 1) for i in range(count - 1)]
        backward = [(target, source) for source, target in forward]
        low = lax.ppermute(
            lax.slice_in_dim(block, block.shape[dim] - width, None, axis=dim), axis, forward
        )
        high = lax.ppermute(lax.slice_in_dim(block, 0, width, axis=dim), axis, backward)
        block = jnp.concatenate([low, block, high], axis=dim)
    return block


def wrapped_diff(delta):
    above = (delta - TWO_PI_HI) - TWO_PI_LO
    below = (delta + TWO_PI_HI) + TWO_PI_LO
    return jnp.where(delta >= PI32, above, jnp.where(delta <= -PI32, below, delta))


def unwrap_kernel(rows_out, ph_ref, wt_ref, top_ref, bot_ref, o_ref, p_ref, q_ref, cur_ref):
    for b in range(ph_ref.shape[0]):
        p_ref[pl.ds(0, HALO), :] = top_ref[0, b]
        p_ref[pl.ds(HALO, rows_out), :] = ph_ref[b]
        p_ref[pl.ds(HALO + rows_out, HALO), :] = bot_ref[0, b]
        q_ref[pl.ds(0, HALO), :] = top_ref[1, b]
        q_ref[pl.ds(HALO, rows_out), :] = wt_ref[b].astype(jnp.float32)
        q_ref[pl.ds(HALO + rows_out, HALO), :] = bot_ref[1, b]
        p = p_ref[...]
        q = q_ref[...]
        nr, nc = p.shape
        row = lax.broadcasted_iota(jnp.int32, (nr, nc), 0)
        col = lax.broadcasted_iota(jnp.int32, (nr, nc), 1)
        zero = jnp.zeros((nr, nc), jnp.float32)
        p_dn = pltpu.roll(p, nr - 1, 0)
        q_dn = pltpu.roll(q, nr - 1, 0)
        g_dn = wrapped_diff(p_dn - p)
        w_dn = jnp.where(row < nr - 1, q_dn * q, zero)
        p_rt = pltpu.roll(p, nc - 1, 1)
        q_rt = pltpu.roll(q, nc - 1, 1)
        g_rt = wrapped_diff(p_rt - p)
        w_rt = jnp.where(col < nc - 1, q_rt * q, zero)
        g_up = pltpu.roll(g_dn, 1, 0)
        w_up = pltpu.roll(w_dn, 1, 0)
        g_lt = pltpu.roll(g_rt, 1, 1)
        w_lt = pltpu.roll(w_rt, 1, 1)
        den = ((w_up + w_dn) + w_lt) + w_rt
        den = jnp.where(den > 0.0, den, 1.0)
        inv = 1.0 / den
        num = w_up * g_up
        num = num - w_dn * g_dn
        num = num + w_lt * g_lt
        num = num - w_rt * g_rt
        const = num * inv
        a_up, a_dn, a_lt, a_rt = w_up * inv, w_dn * inv, w_lt * inv, w_rt * inv
        cur = const
        for _ in range(SWEEPS - 1):
            nxt = const + a_up * pltpu.roll(cur, 1, 0)
            nxt = nxt + a_dn * pltpu.roll(cur, nr - 1, 0)
            nxt = nxt + a_lt * pltpu.roll(cur, 1, 1)
            nxt = nxt + a_rt * pltpu.roll(cur, nc - 1, 1)
            cur = nxt
        cur_ref[...] = cur
        half = rows_out // 2
        upper = cur_ref[pl.ds(HALO, half), :]
        lower = cur_ref[pl.ds(HALO + half, half), :]
        lane = lax.broadcasted_iota(jnp.int32, (half, nc), 1) % 128
        first = lane < 64
        even = jnp.where(first, upper, pltpu.roll(lower, 64, 1))
        odd = jnp.where(first, pltpu.roll(upper, nc - 64, 1), lower)
        for m in range(nc // 128):
            o_ref[2 * m, b] = even[:, 128 * m : 128 * (m + 1)]
            o_ref[2 * m + 1, b] = odd[:, 128 * m : 128 * (m + 1)]


def unwrap(phase, weights, top, bottom):
    n, rows_out, nc = phase.shape
    nr = rows_out + 2 * HALO
    per = 2
    halo_spec = pl.BlockSpec((2, per, HALO, nc), lambda i: (0, i, 0, 0))
    return pl.pallas_call(
        functools.partial(unwrap_kernel, rows_out),
        grid=(n // per,),
        in_specs=[
            pl.BlockSpec((per, rows_out, nc), lambda i: (i, 0, 0)),
            pl.BlockSpec((per, rows_out, nc), lambda i: (i, 0, 0)),
            halo_spec,
            halo_spec,
        ],
        out_specs=pl.BlockSpec((nc // 64, per, rows_out // 2, 128), lambda i: (0, i, 0, 0)),
        out_shape=jax.ShapeDtypeStruct((nc // 64, n, rows_out // 2, 128), jnp.float32),
        scratch_shapes=[pltpu.VMEM((nr, nc), jnp.float32)] * 3,
        cost_estimate=pl.CostEstimate(
            flops=120 * n * nr * nc, bytes_accessed=4 * n * nc * (2 * nr + rows_out), transcendentals=0
        ),
    )(phase, weights, top, bottom)


def invert_kernel(rows, x_ref, pseudo_ref, design_ref, s_ref, r_ref):
    ifg = pseudo_ref.shape[1]
    pseudo = pseudo_ref[...]
    design = design_ref[...]
    for k in range(rows):
        x = x_ref[pl.ds(k, ifg, stride=rows), :]
        series = jnp.dot(pseudo, x, precision=lax.Precision.HIGH, preferred_element_type=jnp.float32)
        fit = jnp.dot(design, series, precision=lax.Precision.HIGH, preferred_element_type=jnp.float32)
        res_t = (x - fit).T
        ser_t = series.T
        r_ref[pl.ds(k * 64, 64), :] = res_t[:64]
        r_ref[pl.ds((k + rows) * 64, 64), :] = res_t[64:]
        s_ref[pl.ds(k * 64, 64), :] = ser_t[:64]
        s_ref[pl.ds((k + rows) * 64, 64), :] = ser_t[64:]


def invert(packed, pseudo, design, rows):
    ifg = pseudo.shape[1]
    epochs = pseudo.shape[0]
    wide = epochs + (-epochs) % 8
    pseudo = jnp.pad(pseudo, ((0, wide - epochs), (0, 0)))
    design = jnp.pad(design, ((0, 0), (0, wide - epochs)))
    whole = pl.BlockSpec(memory_space=pltpu.VMEM)
    series_t, residual_t = pl.pallas_call(
        functools.partial(invert_kernel, rows),
        in_specs=[whole, whole, whole],
        out_specs=(whole, whole),
        out_shape=(
            jax.ShapeDtypeStruct((2 * rows * 64, wide), jnp.float32),
            jax.ShapeDtypeStruct((2 * rows * 64, ifg), jnp.float32),
        ),
        cost_estimate=pl.CostEstimate(
            flops=4 * 6 * wide * ifg * rows * 128,
            bytes_accessed=4 * 128 * rows * (2 * ifg + wide),
            transcendentals=0,
        ),
    )(packed, pseudo, design)
    return series_t[:, :epochs], residual_t


def binomial(padded, axis):
    length = padded.shape[axis] - 4

    def shifted(offset):
        return lax.slice_in_dim(padded, offset, offset + length, axis=axis)

    return (
        shifted(0) + 4.0 * shifted(1) + 6.0 * shifted(2) + 4.0 * shifted(3) + shifted(4)
    ) * 0.0625


def network_maps(network):
    date_ids = jnp.arange(DATES, dtype=jnp.int32)[None, :]
    full = (network[:, 1:2] == date_ids).astype(jnp.float32) - (network[:, 0:1] == date_ids).astype(
        jnp.float32
    )
    design = full[:, 1:]
    normal_matrix = jnp.dot(design.T, design, precision=lax.Precision.HIGHEST)
    factor = jnp.linalg.cholesky(normal_matrix)
    pseudo = jax.scipy.linalg.cho_solve((factor, True), design.T)
    return (design, pseudo)


def on_device(phase, weights, network):
    design, pseudo = network_maps(network)
    rows = phase.shape[1]
    count = lax.axis_size("rows")
    forward = [(i, i + 1) for i in range(count - 1)]
    backward = [(target, source) for source, target in forward]
    edge_low = jnp.stack([phase[:, rows - HALO :], weights[:, rows - HALO :].astype(jnp.float32)])
    edge_high = jnp.stack([phase[:, :HALO], weights[:, :HALO].astype(jnp.float32)])
    top = lax.ppermute(edge_low, "rows", forward)
    bottom = lax.ppermute(edge_high, "rows", backward)
    current = unwrap(phase, weights, top, bottom)
    received = lax.all_to_all(current, "ifg", split_axis=0, concat_axis=0, tiled=True)
    ifg = received.shape[0] * received.shape[1]
    half = rows // 2
    series_t, residual_t = invert(received.reshape(ifg * half, 128), pseudo, design, half)

    def unpack(x):
        return x.reshape(rows, 64, x.shape[1]).transpose(2, 0, 1)

    series_block = unpack(series_t)
    residual = unpack(residual_t)
    padded = extended_2(residual, (("rows", 1), ("ifg", 2)), 2)
    filtered = binomial(binomial(padded, 1), 2)
    return (series_block, filtered.astype(jnp.bfloat16))


def solution(mesh):
    return jax.shard_map(
        on_device,
        mesh=mesh,
        in_specs=(P("ifg", "rows", None), P("ifg", "rows", None), P()),
        out_specs=(P(None, "rows", "ifg"), P(None, "rows", "ifg")),
        check_vma=False,
    )
```

```python
import functools

import numpy as np
import jax
import jax.numpy as jnp
from jax import lax
from jax.experimental import pallas as pl
from jax.experimental.pallas import tpu as pltpu
from jax.sharding import PartitionSpec as P

DATES = 96
SWEEPS = 4
FILTER_HALO = 2
HALO = 8
PI32 = float(np.float32(np.pi))
TWO_PI_HI = float(np.float32(2 * np.pi))
TWO_PI_LO = float(np.float32(2 * np.pi - np.float64(np.float32(2 * np.pi))))


def extended_2(block, sides, width):
    for axis, dim in sides:
        count = lax.axis_size(axis)
        forward = [(i, i + 1) for i in range(count - 1)]
        backward = [(target, source) for source, target in forward]
        low = lax.ppermute(
            lax.slice_in_dim(block, block.shape[dim] - width, None, axis=dim), axis, forward
        )
        high = lax.ppermute(lax.slice_in_dim(block, 0, width, axis=dim), axis, backward)
        block = jnp.concatenate([low, block, high], axis=dim)
    return block


def wrapped_diff(delta):
    above = (delta - TWO_PI_HI) - TWO_PI_LO
    below = (delta + TWO_PI_HI) + TWO_PI_LO
    return jnp.where(delta >= PI32, above, jnp.where(delta <= -PI32, below, delta))


def unwrap_kernel(rows_out, ph_ref, wt_ref, top_ref, bot_ref, o_ref, p_ref, q_ref, cur_ref):
    for b in range(ph_ref.shape[0]):
        p_ref[pl.ds(0, HALO), :] = top_ref[0, b]
        p_ref[pl.ds(HALO, rows_out), :] = ph_ref[b]
        p_ref[pl.ds(HALO + rows_out, HALO), :] = bot_ref[0, b]
        q_ref[pl.ds(0, HALO), :] = top_ref[1, b]
        q_ref[pl.ds(HALO, rows_out), :] = wt_ref[b].astype(jnp.float32)
        q_ref[pl.ds(HALO + rows_out, HALO), :] = bot_ref[1, b]
        p = p_ref[...]
        q = q_ref[...]
        nr, nc = p.shape
        row = lax.broadcasted_iota(jnp.int32, (nr, nc), 0)
        col = lax.broadcasted_iota(jnp.int32, (nr, nc), 1)
        zero = jnp.zeros((nr, nc), jnp.float32)
        p_dn = pltpu.roll(p, nr - 1, 0)
        q_dn = pltpu.roll(q, nr - 1, 0)
        g_dn = wrapped_diff(p_dn - p)
        w_dn = jnp.where(row < nr - 1, q_dn * q, zero)
        p_rt = pltpu.roll(p, nc - 1, 1)
        q_rt = pltpu.roll(q, nc - 1, 1)
        g_rt = wrapped_diff(p_rt - p)
        w_rt = jnp.where(col < nc - 1, q_rt * q, zero)
        g_up = pltpu.roll(g_dn, 1, 0)
        w_up = pltpu.roll(w_dn, 1, 0)
        g_lt = pltpu.roll(g_rt, 1, 1)
        w_lt = pltpu.roll(w_rt, 1, 1)
        den = ((w_up + w_dn) + w_lt) + w_rt
        den = jnp.where(den > 0.0, den, 1.0)
        inv = 1.0 / den
        num = w_up * g_up
        num = num - w_dn * g_dn
        num = num + w_lt * g_lt
        num = num - w_rt * g_rt
        const = num * inv
        a_up, a_dn, a_lt, a_rt = w_up * inv, w_dn * inv, w_lt * inv, w_rt * inv
        cur = const
        for _ in range(SWEEPS - 1):
            nxt = const + a_up * pltpu.roll(cur, 1, 0)
            nxt = nxt + a_dn * pltpu.roll(cur, nr - 1, 0)
            nxt = nxt + a_lt * pltpu.roll(cur, 1, 1)
            nxt = nxt + a_rt * pltpu.roll(cur, nc - 1, 1)
            cur = nxt
        cur_ref[...] = cur
        half = rows_out // 2 + FILTER_HALO
        upper = cur_ref[pl.ds(HALO - FILTER_HALO, half), :]
        lower = cur_ref[pl.ds(HALO - FILTER_HALO + half, half), :]
        lane = lax.broadcasted_iota(jnp.int32, (half, nc), 1) % 128
        first = lane < 64
        even = jnp.where(first, upper, pltpu.roll(lower, 64, 1))
        odd = jnp.where(first, pltpu.roll(upper, nc - 64, 1), lower)
        for m in range(nc // 128):
            o_ref[2 * m, pl.ds(b * half, half), :] = even[:, 128 * m : 128 * (m + 1)]
            o_ref[2 * m + 1, pl.ds(b * half, half), :] = odd[:, 128 * m : 128 * (m + 1)]


def unwrap(phase, weights, top, bottom):
    n, rows_out, nc = phase.shape
    nr = rows_out + 2 * HALO
    per = 4
    half = rows_out // 2 + FILTER_HALO
    halo_spec = pl.BlockSpec((2, per, HALO, nc), lambda i: (0, i, 0, 0))
    return pl.pallas_call(
        functools.partial(unwrap_kernel, rows_out),
        grid=(n // per,),
        in_specs=[
            pl.BlockSpec((per, rows_out, nc), lambda i: (i, 0, 0)),
            pl.BlockSpec((per, rows_out, nc), lambda i: (i, 0, 0)),
            halo_spec,
            halo_spec,
        ],
        out_specs=pl.BlockSpec((nc // 64, per * half, 128), lambda i: (0, i, 0)),
        out_shape=jax.ShapeDtypeStruct((nc // 64, n * half, 128), jnp.float32),
        scratch_shapes=[pltpu.VMEM((nr, nc), jnp.float32)] * 3,
        cost_estimate=pl.CostEstimate(
            flops=120 * n * nr * nc, bytes_accessed=4 * n * nc * (2 * nr + rows_out), transcendentals=0
        ),
    )(phase, weights, top, bottom)


def invert_kernel(rows, x_ref, pseudo_ref, design_ref, s_ref, r_ref):
    ifg = pseudo_ref.shape[1]
    own = rows - FILTER_HALO
    pseudo = pseudo_ref[...]
    design = design_ref[...]
    for k in range(rows):
        x = x_ref[pl.ds(k, ifg, stride=rows), :]
        series = jnp.dot(pseudo, x, precision=lax.Precision.HIGH, preferred_element_type=jnp.float32)
        fit = jnp.dot(design, series, precision=lax.Precision.HIGH, preferred_element_type=jnp.float32)
        res_t = (x - fit).T
        ser_t = series.T
        r_ref[pl.ds(k * 64, 64), :] = res_t[:64]
        r_ref[pl.ds((k + rows) * 64, 64), :] = res_t[64:]
        if k >= FILTER_HALO:
            s_ref[pl.ds((k - FILTER_HALO) * 64, 64), :] = ser_t[:64]
        if k < own:
            s_ref[pl.ds((k + own) * 64, 64), :] = ser_t[64:]


def invert(packed, pseudo, design, rows):
    ifg = pseudo.shape[1]
    epochs = pseudo.shape[0]
    wide = epochs + (-epochs) % 8
    pseudo = jnp.pad(pseudo, ((0, wide - epochs), (0, 0)))
    design = jnp.pad(design, ((0, 0), (0, wide - epochs)))
    whole = pl.BlockSpec(memory_space=pltpu.VMEM)
    series_t, residual_t = pl.pallas_call(
        functools.partial(invert_kernel, rows),
        in_specs=[whole, whole, whole],
        out_specs=(whole, whole),
        out_shape=(
            jax.ShapeDtypeStruct((2 * (rows - FILTER_HALO) * 64, wide), jnp.float32),
            jax.ShapeDtypeStruct((2 * rows * 64, ifg), jnp.float32),
        ),
        cost_estimate=pl.CostEstimate(
            flops=4 * 6 * wide * ifg * rows * 128,
            bytes_accessed=4 * 128 * rows * (2 * ifg + wide),
            transcendentals=0,
        ),
    )(packed, pseudo, design)
    return series_t[:, :epochs], residual_t


def binomial(padded, axis):
    length = padded.shape[axis] - 4

    def shifted(offset):
        return lax.slice_in_dim(padded, offset, offset + length, axis=axis)

    return (
        shifted(0) + 4.0 * shifted(1) + 6.0 * shifted(2) + 4.0 * shifted(3) + shifted(4)
    ) * 0.0625


def network_maps(network):
    date_ids = jnp.arange(DATES, dtype=jnp.int32)[None, :]
    full = (network[:, 1:2] == date_ids).astype(jnp.float32) - (network[:, 0:1] == date_ids).astype(
        jnp.float32
    )
    design = full[:, 1:]
    normal_matrix = jnp.dot(design.T, design, precision=lax.Precision.HIGHEST)
    factor = jnp.linalg.cholesky(normal_matrix)
    pseudo = jax.scipy.linalg.cho_solve((factor, True), design.T)
    return (design, pseudo)


def on_device(phase, weights, network):
    design, pseudo = network_maps(network)
    rows = phase.shape[1]
    count = lax.axis_size("rows")
    forward = [(i, i + 1) for i in range(count - 1)]
    backward = [(target, source) for source, target in forward]
    edge_low = jnp.stack([phase[:, rows - HALO :], weights[:, rows - HALO :].astype(jnp.float32)])
    edge_high = jnp.stack([phase[:, :HALO], weights[:, :HALO].astype(jnp.float32)])
    top = lax.ppermute(edge_low, "rows", forward)
    bottom = lax.ppermute(edge_high, "rows", backward)
    current = unwrap(phase, weights, top, bottom)
    received = lax.all_to_all(current, "ifg", split_axis=0, concat_axis=0, tiled=True)
    half = rows // 2 + FILTER_HALO
    series_t, residual_t = invert(received.reshape(-1, 128), pseudo, design, half)

    def unpack(x):
        return x.reshape(-1, 64, x.shape[1]).transpose(2, 0, 1)

    series_block = unpack(series_t)
    residual = unpack(residual_t)
    padded = extended_2(residual, (("ifg", 2),), FILTER_HALO)
    filtered = binomial(binomial(padded, 1), 2)
    return (series_block, filtered.astype(jnp.bfloat16))


def solution(mesh):
    return jax.shard_map(
        on_device,
        mesh=mesh,
        in_specs=(P("ifg", "rows", None), P("ifg", "rows", None), P()),
        out_specs=(P(None, "rows", "ifg"), P(None, "rows", "ifg")),
        check_vma=False,
    )
```

```python
import functools

import numpy as np
import jax
import jax.numpy as jnp
from jax import lax
from jax.experimental import pallas as pl
from jax.experimental.pallas import tpu as pltpu
from jax.sharding import PartitionSpec as P

DATES = 96
SWEEPS = 4
FILTER_HALO = 2
SENT = SWEEPS + FILTER_HALO
HALO = 8
PI32 = float(np.float32(np.pi))
TWO_PI_HI = float(np.float32(2 * np.pi))
TWO_PI_LO = float(np.float32(2 * np.pi - np.float64(np.float32(2 * np.pi))))


def extended_2(block, sides, width):
    for axis, dim in sides:
        count = lax.axis_size(axis)
        forward = [(i, i + 1) for i in range(count - 1)]
        backward = [(target, source) for source, target in forward]
        low = lax.ppermute(
            lax.slice_in_dim(block, block.shape[dim] - width, None, axis=dim), axis, forward
        )
        high = lax.ppermute(lax.slice_in_dim(block, 0, width, axis=dim), axis, backward)
        block = jnp.concatenate([low, block, high], axis=dim)
    return block


def wrapped_diff(delta):
    above = (delta - TWO_PI_HI) - TWO_PI_LO
    below = (delta + TWO_PI_HI) + TWO_PI_LO
    return jnp.where(delta >= PI32, above, jnp.where(delta <= -PI32, below, delta))


def unwrap_kernel(rows_out, ph_ref, wt_ref, top_ref, bot_ref, o_ref, p_ref, q_ref, cur_ref):
    for b in range(ph_ref.shape[0]):
        spare = HALO - SENT
        blank = jnp.zeros((spare, p_ref.shape[1]), jnp.float32)
        for ref in (p_ref, q_ref):
            ref[pl.ds(0, spare), :] = blank
            ref[pl.ds(HALO + rows_out + SENT, spare), :] = blank
        p_ref[pl.ds(spare, SENT), :] = top_ref[0, b]
        p_ref[pl.ds(HALO, rows_out), :] = ph_ref[b]
        p_ref[pl.ds(HALO + rows_out, SENT), :] = bot_ref[0, b]
        q_ref[pl.ds(spare, SENT), :] = top_ref[1, b]
        q_ref[pl.ds(HALO, rows_out), :] = wt_ref[b].astype(jnp.float32)
        q_ref[pl.ds(HALO + rows_out, SENT), :] = bot_ref[1, b]
        p = p_ref[...]
        q = q_ref[...]
        nr, nc = p.shape
        row = lax.broadcasted_iota(jnp.int32, (nr, nc), 0)
        col = lax.broadcasted_iota(jnp.int32, (nr, nc), 1)
        zero = jnp.zeros((nr, nc), jnp.float32)
        p_dn = pltpu.roll(p, nr - 1, 0)
        q_dn = pltpu.roll(q, nr - 1, 0)
        g_dn = wrapped_diff(p_dn - p)
        w_dn = jnp.where(row < nr - 1, q_dn * q, zero)
        p_rt = pltpu.roll(p, nc - 1, 1)
        q_rt = pltpu.roll(q, nc - 1, 1)
        g_rt = wrapped_diff(p_rt - p)
        w_rt = jnp.where(col < nc - 1, q_rt * q, zero)
        g_up = pltpu.roll(g_dn, 1, 0)
        w_up = pltpu.roll(w_dn, 1, 0)
        g_lt = pltpu.roll(g_rt, 1, 1)
        w_lt = pltpu.roll(w_rt, 1, 1)
        den = ((w_up + w_dn) + w_lt) + w_rt
        den = jnp.where(den > 0.0, den, 1.0)
        inv = 1.0 / den
        num = w_up * g_up
        num = num - w_dn * g_dn
        num = num + w_lt * g_lt
        num = num - w_rt * g_rt
        const = num * inv
        a_up, a_dn, a_lt, a_rt = w_up * inv, w_dn * inv, w_lt * inv, w_rt * inv
        cur = const
        for _ in range(SWEEPS - 1):
            nxt = const + a_up * pltpu.roll(cur, 1, 0)
            nxt = nxt + a_dn * pltpu.roll(cur, nr - 1, 0)
            nxt = nxt + a_lt * pltpu.roll(cur, 1, 1)
            nxt = nxt + a_rt * pltpu.roll(cur, nc - 1, 1)
            cur = nxt
        cur_ref[...] = cur
        half = rows_out // 2 + FILTER_HALO
        upper = cur_ref[pl.ds(HALO - FILTER_HALO, half), :]
        lower = cur_ref[pl.ds(HALO - FILTER_HALO + half, half), :]
        lane = lax.broadcasted_iota(jnp.int32, (half, nc), 1) % 128
        first = lane < 64
        even = jnp.where(first, upper, pltpu.roll(lower, 64, 1))
        odd = jnp.where(first, pltpu.roll(upper, nc - 64, 1), lower)
        for m in range(nc // 128):
            o_ref[2 * m, pl.ds(b * half, half), :] = even[:, 128 * m : 128 * (m + 1)]
            o_ref[2 * m + 1, pl.ds(b * half, half), :] = odd[:, 128 * m : 128 * (m + 1)]


def unwrap(phase, weights, top, bottom):
    n, rows_out, nc = phase.shape
    nr = rows_out + 2 * HALO
    per = 4
    half = rows_out // 2 + FILTER_HALO
    halo_spec = pl.BlockSpec((2, per, SENT, nc), lambda i: (0, i, 0, 0))
    return pl.pallas_call(
        functools.partial(unwrap_kernel, rows_out),
        grid=(n // per,),
        in_specs=[
            pl.BlockSpec((per, rows_out, nc), lambda i: (i, 0, 0)),
            pl.BlockSpec((per, rows_out, nc), lambda i: (i, 0, 0)),
            halo_spec,
            halo_spec,
        ],
        out_specs=pl.BlockSpec((nc // 64, per * half, 128), lambda i: (0, i, 0)),
        out_shape=jax.ShapeDtypeStruct((nc // 64, n * half, 128), jnp.float32),
        scratch_shapes=[pltpu.VMEM((nr, nc), jnp.float32)] * 3,
        cost_estimate=pl.CostEstimate(
            flops=120 * n * nr * nc, bytes_accessed=4 * n * nc * (2 * nr + rows_out), transcendentals=0
        ),
    )(phase, weights, top, bottom)


def invert_kernel(rows, x_ref, pseudo_ref, design_ref, s_ref, r_ref):
    ifg = pseudo_ref.shape[1]
    own = rows - FILTER_HALO
    pseudo = pseudo_ref[...]
    design = design_ref[...]
    for k in range(rows):
        x = x_ref[pl.ds(k, ifg, stride=rows), :]
        series = jnp.dot(pseudo, x, precision=lax.Precision.HIGH, preferred_element_type=jnp.float32)
        fit = jnp.dot(design, series, precision=lax.Precision.HIGH, preferred_element_type=jnp.float32)
        res_t = (x - fit).T
        ser_t = series.T
        r_ref[pl.ds(k * 64, 64), :] = res_t[:64]
        r_ref[pl.ds((k + rows) * 64, 64), :] = res_t[64:]
        if k >= FILTER_HALO:
            s_ref[pl.ds((k - FILTER_HALO) * 64, 64), :] = ser_t[:64]
        if k < own:
            s_ref[pl.ds((k + own) * 64, 64), :] = ser_t[64:]


def invert(packed, pseudo, design, rows):
    ifg = pseudo.shape[1]
    epochs = pseudo.shape[0]
    wide = epochs + (-epochs) % 8
    pseudo = jnp.pad(pseudo, ((0, wide - epochs), (0, 0)))
    design = jnp.pad(design, ((0, 0), (0, wide - epochs)))
    whole = pl.BlockSpec(memory_space=pltpu.VMEM)
    series_t, residual_t = pl.pallas_call(
        functools.partial(invert_kernel, rows),
        in_specs=[whole, whole, whole],
        out_specs=(whole, whole),
        out_shape=(
            jax.ShapeDtypeStruct((2 * (rows - FILTER_HALO) * 64, wide), jnp.float32),
            jax.ShapeDtypeStruct((2 * rows * 64, ifg), jnp.float32),
        ),
        cost_estimate=pl.CostEstimate(
            flops=4 * 6 * wide * ifg * rows * 128,
            bytes_accessed=4 * 128 * rows * (2 * ifg + wide),
            transcendentals=0,
        ),
    )(packed, pseudo, design)
    return series_t[:, :epochs], residual_t


def binomial(padded, axis):
    length = padded.shape[axis] - 4

    def shifted(offset):
        return lax.slice_in_dim(padded, offset, offset + length, axis=axis)

    return (
        shifted(0) + 4.0 * shifted(1) + 6.0 * shifted(2) + 4.0 * shifted(3) + shifted(4)
    ) * 0.0625


def network_maps(network):
    date_ids = jnp.arange(DATES, dtype=jnp.int32)[None, :]
    full = (network[:, 1:2] == date_ids).astype(jnp.float32) - (network[:, 0:1] == date_ids).astype(
        jnp.float32
    )
    design = full[:, 1:]
    normal_matrix = jnp.dot(design.T, design, precision=lax.Precision.HIGHEST)
    factor = jnp.linalg.cholesky(normal_matrix)
    pseudo = jax.scipy.linalg.cho_solve((factor, True), design.T)
    return (design, pseudo)


def on_device(phase, weights, network):
    design, pseudo = network_maps(network)
    rows = phase.shape[1]
    count = lax.axis_size("rows")
    forward = [(i, i + 1) for i in range(count - 1)]
    backward = [(target, source) for source, target in forward]
    edge_low = jnp.stack([phase[:, rows - SENT :], weights[:, rows - SENT :].astype(jnp.float32)])
    edge_high = jnp.stack([phase[:, :SENT], weights[:, :SENT].astype(jnp.float32)])
    top = lax.ppermute(edge_low, "rows", forward)
    bottom = lax.ppermute(edge_high, "rows", backward)
    current = unwrap(phase, weights, top, bottom)
    received = lax.all_to_all(current, "ifg", split_axis=0, concat_axis=0, tiled=True)
    half = rows // 2 + FILTER_HALO
    series_t, residual_t = invert(received.reshape(-1, 128), pseudo, design, half)

    def unpack(x):
        return x.reshape(-1, 64, x.shape[1]).transpose(2, 0, 1)

    series_block = unpack(series_t)
    residual = unpack(residual_t)
    padded = extended_2(residual, (("ifg", 2),), FILTER_HALO)
    filtered = binomial(binomial(padded, 1), 2)
    return (series_block, filtered.astype(jnp.bfloat16))


def solution(mesh):
    return jax.shard_map(
        on_device,
        mesh=mesh,
        in_specs=(P("ifg", "rows", None), P("ifg", "rows", None), P()),
        out_specs=(P(None, "rows", "ifg"), P(None, "rows", "ifg")),
        check_vma=False,
    )
```

```python
import functools

import numpy as np
import jax
import jax.numpy as jnp
from jax import lax
from jax.experimental import pallas as pl
from jax.experimental.pallas import tpu as pltpu
from jax.sharding import PartitionSpec as P

DATES = 96
SWEEPS = 4
FILTER_HALO = 2
SENT = SWEEPS + FILTER_HALO
HALO = 8
PI32 = float(np.float32(np.pi))
TWO_PI_HI = float(np.float32(2 * np.pi))
TWO_PI_LO = float(np.float32(2 * np.pi - np.float64(np.float32(2 * np.pi))))


def extended_2(block, sides, width):
    for axis, dim in sides:
        count = lax.axis_size(axis)
        forward = [(i, i + 1) for i in range(count - 1)]
        backward = [(target, source) for source, target in forward]
        low = lax.ppermute(
            lax.slice_in_dim(block, block.shape[dim] - width, None, axis=dim), axis, forward
        )
        high = lax.ppermute(lax.slice_in_dim(block, 0, width, axis=dim), axis, backward)
        block = jnp.concatenate([low, block, high], axis=dim)
    return block


def wrapped_diff(delta):
    above = (delta - TWO_PI_HI) - TWO_PI_LO
    below = (delta + TWO_PI_HI) + TWO_PI_LO
    return jnp.where(delta >= PI32, above, jnp.where(delta <= -PI32, below, delta))


def unwrap_kernel(rows_out, ph_ref, wt_ref, top_ref, bot_ref, o_ref, p_ref, q_ref, cur_ref):
    for b in range(ph_ref.shape[0]):
        spare = HALO - SENT
        blank = jnp.zeros((spare, p_ref.shape[1]), jnp.float32)
        for ref in (p_ref, q_ref):
            ref[pl.ds(0, spare), :] = blank
            ref[pl.ds(HALO + rows_out + SENT, spare), :] = blank
        p_ref[pl.ds(spare, SENT), :] = top_ref[0, b]
        p_ref[pl.ds(HALO, rows_out), :] = ph_ref[b]
        p_ref[pl.ds(HALO + rows_out, SENT), :] = bot_ref[0, b]
        q_ref[pl.ds(spare, SENT), :] = top_ref[1, b]
        q_ref[pl.ds(HALO, rows_out), :] = wt_ref[b].astype(jnp.float32)
        q_ref[pl.ds(HALO + rows_out, SENT), :] = bot_ref[1, b]
        p = p_ref[...]
        q = q_ref[...]
        nr, nc = p.shape
        row = lax.broadcasted_iota(jnp.int32, (nr, nc), 0)
        col = lax.broadcasted_iota(jnp.int32, (nr, nc), 1)
        zero = jnp.zeros((nr, nc), jnp.float32)
        p_dn = pltpu.roll(p, nr - 1, 0)
        q_dn = pltpu.roll(q, nr - 1, 0)
        g_dn = wrapped_diff(p_dn - p)
        w_dn = jnp.where(row < nr - 1, q_dn * q, zero)
        p_rt = pltpu.roll(p, nc - 1, 1)
        q_rt = pltpu.roll(q, nc - 1, 1)
        g_rt = wrapped_diff(p_rt - p)
        w_rt = jnp.where(col < nc - 1, q_rt * q, zero)
        g_up = pltpu.roll(g_dn, 1, 0)
        w_up = pltpu.roll(w_dn, 1, 0)
        g_lt = pltpu.roll(g_rt, 1, 1)
        w_lt = pltpu.roll(w_rt, 1, 1)
        den = ((w_up + w_dn) + w_lt) + w_rt
        den = jnp.where(den > 0.0, den, 1.0)
        inv = 1.0 / den
        num = w_up * g_up
        num = num - w_dn * g_dn
        num = num + w_lt * g_lt
        num = num - w_rt * g_rt
        const = num * inv
        a_up, a_dn, a_lt, a_rt = w_up * inv, w_dn * inv, w_lt * inv, w_rt * inv
        cur = const
        for _ in range(SWEEPS - 1):
            nxt = const + a_up * pltpu.roll(cur, 1, 0)
            nxt = nxt + a_dn * pltpu.roll(cur, nr - 1, 0)
            nxt = nxt + a_lt * pltpu.roll(cur, 1, 1)
            nxt = nxt + a_rt * pltpu.roll(cur, nc - 1, 1)
            cur = nxt
        cur_ref[...] = cur
        half = rows_out // 2 + FILTER_HALO
        upper = cur_ref[pl.ds(HALO - FILTER_HALO, half), :]
        lower = cur_ref[pl.ds(HALO - FILTER_HALO + half, half), :]
        lane = lax.broadcasted_iota(jnp.int32, (half, nc), 1) % 128
        first = lane < 64
        even = jnp.where(first, upper, pltpu.roll(lower, 64, 1))
        odd = jnp.where(first, pltpu.roll(upper, nc - 64, 1), lower)
        for m in range(nc // 128):
            o_ref[2 * m, pl.ds(b * half, half), :] = even[:, 128 * m : 128 * (m + 1)]
            o_ref[2 * m + 1, pl.ds(b * half, half), :] = odd[:, 128 * m : 128 * (m + 1)]


def unwrap(phase, weights, top, bottom, part, earlier=None):
    n, rows_out, nc = phase.shape
    nr = rows_out + 2 * HALO
    per = top.shape[1]
    half = rows_out // 2 + FILTER_HALO
    halo_spec = pl.BlockSpec((2, per, SENT, nc), lambda i: (0, 0, 0, 0))
    in_specs = [
        pl.BlockSpec((per, rows_out, nc), lambda i: (part, 0, 0)),
        pl.BlockSpec((per, rows_out, nc), lambda i: (part, 0, 0)),
        halo_spec,
        halo_spec,
    ]
    operands = [phase, weights, top, bottom]
    aliases = {}
    kernel = functools.partial(unwrap_kernel, rows_out)
    if earlier is not None:
        in_specs.append(pl.BlockSpec(memory_space=pl.ANY))
        operands.append(earlier)
        aliases = {4: 0}

        def kernel(ph_ref, wt_ref, top_ref, bot_ref, earlier_ref, o_ref, p_ref, q_ref, cur_ref):
            unwrap_kernel(rows_out, ph_ref, wt_ref, top_ref, bot_ref, o_ref, p_ref, q_ref, cur_ref)

    return pl.pallas_call(
        kernel,
        grid=(1,),
        in_specs=in_specs,
        out_specs=pl.BlockSpec((nc // 64, per * half, 128), lambda i: (0, part, 0)),
        out_shape=jax.ShapeDtypeStruct((nc // 64, n * half, 128), jnp.float32),
        scratch_shapes=[pltpu.VMEM((nr, nc), jnp.float32)] * 3,
        input_output_aliases=aliases,
        cost_estimate=pl.CostEstimate(
            flops=120 * per * nr * nc, bytes_accessed=4 * per * nc * (2 * nr + rows_out), transcendentals=0
        ),
    )(*operands)


def invert_kernel(rows, x_ref, pseudo_ref, design_ref, s_ref, r_ref):
    ifg = pseudo_ref.shape[1]
    own = rows - FILTER_HALO
    pseudo = pseudo_ref[...]
    design = design_ref[...]
    for k in range(rows):
        x = x_ref[pl.ds(k, ifg, stride=rows), :]
        series = jnp.dot(pseudo, x, precision=lax.Precision.HIGH, preferred_element_type=jnp.float32)
        fit = jnp.dot(design, series, precision=lax.Precision.HIGH, preferred_element_type=jnp.float32)
        res_t = (x - fit).T
        ser_t = series.T
        r_ref[pl.ds(k * 64, 64), :] = res_t[:64]
        r_ref[pl.ds((k + rows) * 64, 64), :] = res_t[64:]
        if k >= FILTER_HALO:
            s_ref[pl.ds((k - FILTER_HALO) * 64, 64), :] = ser_t[:64]
        if k < own:
            s_ref[pl.ds((k + own) * 64, 64), :] = ser_t[64:]


def invert(packed, pseudo, design, rows):
    ifg = pseudo.shape[1]
    epochs = pseudo.shape[0]
    wide = epochs + (-epochs) % 8
    pseudo = jnp.pad(pseudo, ((0, wide - epochs), (0, 0)))
    design = jnp.pad(design, ((0, 0), (0, wide - epochs)))
    whole = pl.BlockSpec(memory_space=pltpu.VMEM)
    series_t, residual_t = pl.pallas_call(
        functools.partial(invert_kernel, rows),
        in_specs=[whole, whole, whole],
        out_specs=(whole, whole),
        out_shape=(
            jax.ShapeDtypeStruct((2 * (rows - FILTER_HALO) * 64, wide), jnp.float32),
            jax.ShapeDtypeStruct((2 * rows * 64, ifg), jnp.float32),
        ),
        cost_estimate=pl.CostEstimate(
            flops=4 * 6 * wide * ifg * rows * 128,
            bytes_accessed=4 * 128 * rows * (2 * ifg + wide),
            transcendentals=0,
        ),
    )(packed, pseudo, design)
    return series_t[:, :epochs], residual_t


def binomial(padded, axis):
    length = padded.shape[axis] - 4

    def shifted(offset):
        return lax.slice_in_dim(padded, offset, offset + length, axis=axis)

    return (
        shifted(0) + 4.0 * shifted(1) + 6.0 * shifted(2) + 4.0 * shifted(3) + shifted(4)
    ) * 0.0625


def network_maps(network):
    date_ids = jnp.arange(DATES, dtype=jnp.int32)[None, :]
    full = (network[:, 1:2] == date_ids).astype(jnp.float32) - (network[:, 0:1] == date_ids).astype(
        jnp.float32
    )
    design = full[:, 1:]
    normal_matrix = jnp.dot(design.T, design, precision=lax.Precision.HIGHEST)
    factor = jnp.linalg.cholesky(normal_matrix)
    pseudo = jax.scipy.linalg.cho_solve((factor, True), design.T)
    return (design, pseudo)


def on_device(phase, weights, network):
    design, pseudo = network_maps(network)
    rows = phase.shape[1]
    count = lax.axis_size("rows")
    forward = [(i, i + 1) for i in range(count - 1)]
    backward = [(target, source) for source, target in forward]
    edge_low = jnp.stack([phase[:, rows - SENT :], weights[:, rows - SENT :].astype(jnp.float32)])
    edge_high = jnp.stack([phase[:, :SENT], weights[:, :SENT].astype(jnp.float32)])
    per = phase.shape[0] // 2
    current = None
    for part in range(2):
        top = lax.ppermute(edge_low[:, part * per : (part + 1) * per], "rows", forward)
        bottom = lax.ppermute(edge_high[:, part * per : (part + 1) * per], "rows", backward)
        current = unwrap(phase, weights, top, bottom, part, current)
    received = lax.all_to_all(current, "ifg", split_axis=0, concat_axis=0, tiled=True)
    half = rows // 2 + FILTER_HALO
    series_t, residual_t = invert(received.reshape(-1, 128), pseudo, design, half)

    def unpack(x):
        return x.reshape(-1, 64, x.shape[1]).transpose(2, 0, 1)

    series_block = unpack(series_t)
    residual = unpack(residual_t)
    padded = extended_2(residual, (("ifg", 2),), FILTER_HALO)
    filtered = binomial(binomial(padded, 1), 2)
    return (series_block, filtered.astype(jnp.bfloat16))


def solution(mesh):
    return jax.shard_map(
        on_device,
        mesh=mesh,
        in_specs=(P("ifg", "rows", None), P("ifg", "rows", None), P()),
        out_specs=(P(None, "rows", "ifg"), P(None, "rows", "ifg")),
        check_vma=False,
    )
```

```python
import functools

import numpy as np
import jax
import jax.numpy as jnp
from jax import lax
from jax.experimental import pallas as pl
from jax.experimental.pallas import tpu as pltpu
from jax.sharding import PartitionSpec as P

DATES = 96
SWEEPS = 4
FILTER_HALO = 2
HALO = 8
PI32 = float(np.float32(np.pi))
TWO_PI_HI = float(np.float32(2 * np.pi))
TWO_PI_LO = float(np.float32(2 * np.pi - np.float64(np.float32(2 * np.pi))))


def extended_2(block, sides, width):
    for axis, dim in sides:
        count = lax.axis_size(axis)
        forward = [(i, i + 1) for i in range(count - 1)]
        backward = [(target, source) for source, target in forward]
        low = lax.ppermute(
            lax.slice_in_dim(block, block.shape[dim] - width, None, axis=dim), axis, forward
        )
        high = lax.ppermute(lax.slice_in_dim(block, 0, width, axis=dim), axis, backward)
        block = jnp.concatenate([low, block, high], axis=dim)
    return block


def wrapped_diff(delta):
    above = (delta - TWO_PI_HI) - TWO_PI_LO
    below = (delta + TWO_PI_HI) + TWO_PI_LO
    return jnp.where(delta >= PI32, above, jnp.where(delta <= -PI32, below, delta))


def unwrap_kernel(rows_out, ph_ref, wt_ref, top_ref, bot_ref, o_ref, p_ref, q_ref, cur_ref):
    for b in range(ph_ref.shape[0]):
        p_ref[pl.ds(0, HALO), :] = top_ref[0, b]
        p_ref[pl.ds(HALO, rows_out), :] = ph_ref[b]
        p_ref[pl.ds(HALO + rows_out, HALO), :] = bot_ref[0, b]
        q_ref[pl.ds(0, HALO), :] = top_ref[1, b]
        q_ref[pl.ds(HALO, rows_out), :] = wt_ref[b].astype(jnp.float32)
        q_ref[pl.ds(HALO + rows_out, HALO), :] = bot_ref[1, b]
        p = p_ref[...]
        q = q_ref[...]
        nr, nc = p.shape
        row = lax.broadcasted_iota(jnp.int32, (nr, nc), 0)
        col = lax.broadcasted_iota(jnp.int32, (nr, nc), 1)
        zero = jnp.zeros((nr, nc), jnp.float32)
        p_dn = pltpu.roll(p, nr - 1, 0)
        q_dn = pltpu.roll(q, nr - 1, 0)
        g_dn = wrapped_diff(p_dn - p)
        w_dn = jnp.where(row < nr - 1, q_dn * q, zero)
        p_rt = pltpu.roll(p, nc - 1, 1)
        q_rt = pltpu.roll(q, nc - 1, 1)
        g_rt = wrapped_diff(p_rt - p)
        w_rt = jnp.where(col < nc - 1, q_rt * q, zero)
        g_up = pltpu.roll(g_dn, 1, 0)
        w_up = pltpu.roll(w_dn, 1, 0)
        g_lt = pltpu.roll(g_rt, 1, 1)
        w_lt = pltpu.roll(w_rt, 1, 1)
        den = ((w_up + w_dn) + w_lt) + w_rt
        den = jnp.where(den > 0.0, den, 1.0)
        inv = 1.0 / den
        num = w_up * g_up
        num = num - w_dn * g_dn
        num = num + w_lt * g_lt
        num = num - w_rt * g_rt
        const = num * inv
        a_up, a_dn, a_lt, a_rt = w_up * inv, w_dn * inv, w_lt * inv, w_rt * inv
        cur = const
        for _ in range(SWEEPS - 1):
            nxt = const + a_up * pltpu.roll(cur, 1, 0)
            nxt = nxt + a_dn * pltpu.roll(cur, nr - 1, 0)
            nxt = nxt + a_lt * pltpu.roll(cur, 1, 1)
            nxt = nxt + a_rt * pltpu.roll(cur, nc - 1, 1)
            cur = nxt
        cur_ref[...] = cur
        half = rows_out // 2 + FILTER_HALO
        upper = cur_ref[pl.ds(HALO - FILTER_HALO, half), :]
        lower = cur_ref[pl.ds(HALO - FILTER_HALO + half, half), :]
        lane = lax.broadcasted_iota(jnp.int32, (half, nc), 1) % 128
        first = lane < 64
        even = jnp.where(first, upper, pltpu.roll(lower, 64, 1))
        odd = jnp.where(first, pltpu.roll(upper, nc - 64, 1), lower)
        for m in range(nc // 128):
            o_ref[2 * m, pl.ds(b * half, half), :] = even[:, 128 * m : 128 * (m + 1)]
            o_ref[2 * m + 1, pl.ds(b * half, half), :] = odd[:, 128 * m : 128 * (m + 1)]


def unwrap(phase, weights, top, bottom):
    n, rows_out, nc = phase.shape
    nr = rows_out + 2 * HALO
    per = 4
    half = rows_out // 2 + FILTER_HALO
    halo_spec = pl.BlockSpec((2, per, HALO, nc), lambda i: (0, i, 0, 0))
    return pl.pallas_call(
        functools.partial(unwrap_kernel, rows_out),
        grid=(n // per,),
        in_specs=[
            pl.BlockSpec((per, rows_out, nc), lambda i: (i, 0, 0)),
            pl.BlockSpec((per, rows_out, nc), lambda i: (i, 0, 0)),
            halo_spec,
            halo_spec,
        ],
        out_specs=pl.BlockSpec((nc // 64, per * half, 128), lambda i: (0, i, 0)),
        out_shape=jax.ShapeDtypeStruct((nc // 64, n * half, 128), jnp.float32),
        scratch_shapes=[pltpu.VMEM((nr, nc), jnp.float32)] * 3,
        cost_estimate=pl.CostEstimate(
            flops=120 * n * nr * nc, bytes_accessed=4 * n * nc * (2 * nr + rows_out), transcendentals=0
        ),
    )(phase, weights, top, bottom)


def invert_kernel(rows, x_ref, pseudo_in, design_in, s_ref, r_ref, pseudo_ref, design_ref):
    ifg = pseudo_ref.shape[1]
    own = rows - FILTER_HALO
    epochs = pseudo_in.shape[0]
    pseudo_ref[...] = jnp.zeros(pseudo_ref.shape, jnp.float32)
    design_ref[...] = jnp.zeros(design_ref.shape, jnp.float32)
    pseudo_ref[pl.ds(0, epochs), :] = pseudo_in[...]
    design_ref[:, pl.ds(0, epochs)] = design_in[...]
    pseudo = pseudo_ref[...]
    design = design_ref[...]
    for k in range(rows):
        x = x_ref[pl.ds(k, ifg, stride=rows), :]
        series = jnp.dot(pseudo, x, precision=lax.Precision.HIGH, preferred_element_type=jnp.float32)
        fit = jnp.dot(design, series, precision=lax.Precision.HIGH, preferred_element_type=jnp.float32)
        res_t = (x - fit).T
        ser_t = series.T
        r_ref[pl.ds(k * 64, 64), :] = res_t[:64]
        r_ref[pl.ds((k + rows) * 64, 64), :] = res_t[64:]
        if k >= FILTER_HALO:
            s_ref[pl.ds((k - FILTER_HALO) * 64, 64), :] = ser_t[:64]
        if k < own:
            s_ref[pl.ds((k + own) * 64, 64), :] = ser_t[64:]


def invert(packed, pseudo, design, rows):
    ifg = pseudo.shape[1]
    epochs = pseudo.shape[0]
    wide = epochs + (-epochs) % 8
    whole = pl.BlockSpec(memory_space=pltpu.VMEM)
    series_t, residual_t = pl.pallas_call(
        functools.partial(invert_kernel, rows),
        in_specs=[whole, whole, whole],
        out_specs=(whole, whole),
        scratch_shapes=[pltpu.VMEM((wide, ifg), jnp.float32), pltpu.VMEM((ifg, wide), jnp.float32)],
        out_shape=(
            jax.ShapeDtypeStruct((2 * (rows - FILTER_HALO) * 64, wide), jnp.float32),
            jax.ShapeDtypeStruct((2 * rows * 64, ifg), jnp.float32),
        ),
        cost_estimate=pl.CostEstimate(
            flops=4 * 6 * wide * ifg * rows * 128,
            bytes_accessed=4 * 128 * rows * (2 * ifg + wide),
            transcendentals=0,
        ),
    )(packed, pseudo, design)
    return series_t[:, :epochs], residual_t


def binomial(padded, axis):
    length = padded.shape[axis] - 4

    def shifted(offset):
        return lax.slice_in_dim(padded, offset, offset + length, axis=axis)

    return (
        shifted(0) + 4.0 * shifted(1) + 6.0 * shifted(2) + 4.0 * shifted(3) + shifted(4)
    ) * 0.0625


def network_maps(network):
    date_ids = jnp.arange(DATES, dtype=jnp.int32)[None, :]
    full = (network[:, 1:2] == date_ids).astype(jnp.float32) - (network[:, 0:1] == date_ids).astype(
        jnp.float32
    )
    design = full[:, 1:]
    normal_matrix = jnp.dot(design.T, design, precision=lax.Precision.HIGHEST)
    factor = jnp.linalg.cholesky(normal_matrix)
    pseudo = jax.scipy.linalg.cho_solve((factor, True), design.T)
    return (design, pseudo)


def on_device(phase, weights, network):
    design, pseudo = network_maps(network)
    rows = phase.shape[1]
    count = lax.axis_size("rows")
    forward = [(i, i + 1) for i in range(count - 1)]
    backward = [(target, source) for source, target in forward]
    edge_low = jnp.stack([phase[:, rows - HALO :], weights[:, rows - HALO :].astype(jnp.float32)])
    edge_high = jnp.stack([phase[:, :HALO], weights[:, :HALO].astype(jnp.float32)])
    top = lax.ppermute(edge_low, "rows", forward)
    bottom = lax.ppermute(edge_high, "rows", backward)
    current = unwrap(phase, weights, top, bottom)
    received = lax.all_to_all(current, "ifg", split_axis=0, concat_axis=0, tiled=True)
    half = rows // 2 + FILTER_HALO
    series_t, residual_t = invert(received.reshape(-1, 128), pseudo, design, half)

    def unpack(x):
        return x.reshape(-1, 64, x.shape[1]).transpose(2, 0, 1)

    series_block = unpack(series_t)
    residual = unpack(residual_t)
    padded = extended_2(residual, (("ifg", 2),), FILTER_HALO)
    filtered = binomial(binomial(padded, 1), 2)
    return (series_block, filtered.astype(jnp.bfloat16))


def solution(mesh):
    return jax.shard_map(
        on_device,
        mesh=mesh,
        in_specs=(P("ifg", "rows", None), P("ifg", "rows", None), P()),
        out_specs=(P(None, "rows", "ifg"), P(None, "rows", "ifg")),
        check_vma=False,
    )
```

```python
import functools

import numpy as np
import jax
import jax.numpy as jnp
from jax import lax
from jax.experimental import pallas as pl
from jax.experimental.pallas import tpu as pltpu
from jax.sharding import PartitionSpec as P

DATES = 96
SWEEPS = 4
FILTER_HALO = 2
HALO = 8
PI32 = float(np.float32(np.pi))
TWO_PI_HI = float(np.float32(2 * np.pi))
TWO_PI_LO = float(np.float32(2 * np.pi - np.float64(np.float32(2 * np.pi))))


def extended_2(block, sides, width):
    for axis, dim in sides:
        count = lax.axis_size(axis)
        forward = [(i, i + 1) for i in range(count - 1)]
        backward = [(target, source) for source, target in forward]
        low = lax.ppermute(
            lax.slice_in_dim(block, block.shape[dim] - width, None, axis=dim), axis, forward
        )
        high = lax.ppermute(lax.slice_in_dim(block, 0, width, axis=dim), axis, backward)
        block = jnp.concatenate([low, block, high], axis=dim)
    return block


def wrapped_diff(delta):
    above = (delta - TWO_PI_HI) - TWO_PI_LO
    below = (delta + TWO_PI_HI) + TWO_PI_LO
    return jnp.where(delta >= PI32, above, jnp.where(delta <= -PI32, below, delta))


def unwrap_kernel(rows_out, ph_ref, wt_ref, top_ref, bot_ref, o_ref, p_ref, q_ref, cur_ref):
    for b in range(ph_ref.shape[0]):
        p_ref[pl.ds(0, HALO), :] = top_ref[0, b]
        p_ref[pl.ds(HALO, rows_out), :] = ph_ref[b]
        p_ref[pl.ds(HALO + rows_out, HALO), :] = bot_ref[0, b]
        q_ref[pl.ds(0, HALO), :] = top_ref[1, b]
        q_ref[pl.ds(HALO, rows_out), :] = wt_ref[b].astype(jnp.float32)
        q_ref[pl.ds(HALO + rows_out, HALO), :] = bot_ref[1, b]
        p = p_ref[...]
        q = q_ref[...]
        nr, nc = p.shape
        row = lax.broadcasted_iota(jnp.int32, (nr, nc), 0)
        col = lax.broadcasted_iota(jnp.int32, (nr, nc), 1)
        zero = jnp.zeros((nr, nc), jnp.float32)
        p_dn = pltpu.roll(p, nr - 1, 0)
        q_dn = pltpu.roll(q, nr - 1, 0)
        g_dn = wrapped_diff(p_dn - p)
        w_dn = jnp.where(row < nr - 1, q_dn * q, zero)
        p_rt = pltpu.roll(p, nc - 1, 1)
        q_rt = pltpu.roll(q, nc - 1, 1)
        g_rt = wrapped_diff(p_rt - p)
        w_rt = jnp.where(col < nc - 1, q_rt * q, zero)
        g_up = pltpu.roll(g_dn, 1, 0)
        w_up = pltpu.roll(w_dn, 1, 0)
        g_lt = pltpu.roll(g_rt, 1, 1)
        w_lt = pltpu.roll(w_rt, 1, 1)
        den = ((w_up + w_dn) + w_lt) + w_rt
        den = jnp.where(den > 0.0, den, 1.0)
        inv = 1.0 / den
        num = w_up * g_up
        num = num - w_dn * g_dn
        num = num + w_lt * g_lt
        num = num - w_rt * g_rt
        const = num * inv
        a_up, a_dn, a_lt, a_rt = w_up * inv, w_dn * inv, w_lt * inv, w_rt * inv
        cur = const
        for _ in range(SWEEPS - 1):
            nxt = const + a_up * pltpu.roll(cur, 1, 0)
            nxt = nxt + a_dn * pltpu.roll(cur, nr - 1, 0)
            nxt = nxt + a_lt * pltpu.roll(cur, 1, 1)
            nxt = nxt + a_rt * pltpu.roll(cur, nc - 1, 1)
            cur = nxt
        cur_ref[...] = cur
        half = rows_out // 2 + FILTER_HALO
        upper = cur_ref[pl.ds(HALO - FILTER_HALO, half), :]
        lower = cur_ref[pl.ds(HALO - FILTER_HALO + half, half), :]
        lane = lax.broadcasted_iota(jnp.int32, (half, nc), 1) % 128
        first = lane < 64
        even = jnp.where(first, upper, pltpu.roll(lower, 64, 1))
        odd = jnp.where(first, pltpu.roll(upper, nc - 64, 1), lower)
        for m in range(nc // 128):
            o_ref[2 * m, pl.ds(b * half, half), :] = even[:, 128 * m : 128 * (m + 1)]
            o_ref[2 * m + 1, pl.ds(b * half, half), :] = odd[:, 128 * m : 128 * (m + 1)]


def unwrap(phase, weights, top, bottom):
    n, rows_out, nc = phase.shape
    nr = rows_out + 2 * HALO
    per = 4
    half = rows_out // 2 + FILTER_HALO
    halo_spec = pl.BlockSpec((2, per, HALO, nc), lambda i: (0, i, 0, 0))
    return pl.pallas_call(
        functools.partial(unwrap_kernel, rows_out),
        grid=(n // per,),
        in_specs=[
            pl.BlockSpec((per, rows_out, nc), lambda i: (i, 0, 0)),
            pl.BlockSpec((per, rows_out, nc), lambda i: (i, 0, 0)),
            halo_spec,
            halo_spec,
        ],
        out_specs=pl.BlockSpec((nc // 64, per * half, 128), lambda i: (0, i, 0)),
        out_shape=jax.ShapeDtypeStruct((nc // 64, n * half, 128), jnp.float32),
        scratch_shapes=[pltpu.VMEM((nr, nc), jnp.float32)] * 3,
        cost_estimate=pl.CostEstimate(
            flops=120 * n * nr * nc, bytes_accessed=4 * n * nc * (2 * nr + rows_out), transcendentals=0
        ),
    )(phase, weights, top, bottom)


def invert_kernel(rows, x_ref, pseudo_in, design_in, s_ref, r_ref, pseudo_ref, design_ref):
    ifg = pseudo_ref.shape[1]
    own = rows - FILTER_HALO
    epochs = pseudo_in.shape[0]
    pseudo_ref[...] = jnp.zeros(pseudo_ref.shape, jnp.float32)
    design_ref[...] = jnp.zeros(design_ref.shape, jnp.float32)
    pseudo_ref[pl.ds(0, epochs), :] = pseudo_in[...]
    design_ref[:, pl.ds(0, epochs)] = design_in[...]
    pseudo = pseudo_ref[...]
    design = design_ref[...]
    for k in range(rows):
        x = x_ref[pl.ds(k, ifg, stride=rows), :]
        series = jnp.dot(pseudo, x, precision=lax.Precision.HIGH, preferred_element_type=jnp.float32)
        fit = jnp.dot(design, series, precision=lax.Precision.HIGH, preferred_element_type=jnp.float32)
        res_t = (x - fit).T
        ser_t = series.T
        r_ref[pl.ds(k * 64, 64), :] = res_t[:64]
        r_ref[pl.ds((k + rows) * 64, 64), :] = res_t[64:]
        if k >= FILTER_HALO:
            s_ref[pl.ds((k - FILTER_HALO) * 64, 64), :] = ser_t[:64]
        if k < own:
            s_ref[pl.ds((k + own) * 64, 64), :] = ser_t[64:]


def invert(packed, pseudo, design, rows):
    ifg = pseudo.shape[1]
    epochs = pseudo.shape[0]
    wide = epochs + (-epochs) % 8
    whole = pl.BlockSpec(memory_space=pltpu.VMEM)
    series_t, residual_t = pl.pallas_call(
        functools.partial(invert_kernel, rows),
        in_specs=[whole, whole, whole],
        out_specs=(whole, whole),
        scratch_shapes=[pltpu.VMEM((wide, ifg), jnp.float32), pltpu.VMEM((ifg, wide), jnp.float32)],
        out_shape=(
            jax.ShapeDtypeStruct((2 * (rows - FILTER_HALO) * 64, wide), jnp.float32),
            jax.ShapeDtypeStruct((2 * rows * 64, ifg), jnp.float32),
        ),
        cost_estimate=pl.CostEstimate(
            flops=4 * 6 * wide * ifg * rows * 128,
            bytes_accessed=4 * 128 * rows * (2 * ifg + wide),
            transcendentals=0,
        ),
    )(packed, pseudo, design)
    return series_t[:, :epochs], residual_t


def filter_kernel(res_ref, left_ref, right_ref, o_ref, pad_ref, rows_ref):
    n_rows, n_cols = o_ref.shape[0], o_ref.shape[1]
    h = FILTER_HALO
    pad_ref[:, pl.ds(0, h), :] = left_ref[...]
    pad_ref[:, pl.ds(h, n_cols), :] = res_ref[...]
    pad_ref[:, pl.ds(h + n_cols, h), :] = right_ref[...]

    def tap(ref, offset, axis, length):
        if axis == 0:
            return ref[pl.ds(offset, length)]
        return ref[:, pl.ds(offset, length), :]

    rows_ref[...] = (
        tap(pad_ref, 0, 0, n_rows) + 4.0 * tap(pad_ref, 1, 0, n_rows) + 6.0 * tap(pad_ref, 2, 0, n_rows)
        + 4.0 * tap(pad_ref, 3, 0, n_rows) + tap(pad_ref, 4, 0, n_rows)
    ) * 0.0625
    out = (
        tap(rows_ref, 0, 1, n_cols) + 4.0 * tap(rows_ref, 1, 1, n_cols) + 6.0 * tap(rows_ref, 2, 1, n_cols)
        + 4.0 * tap(rows_ref, 3, 1, n_cols) + tap(rows_ref, 4, 1, n_cols)
    ) * 0.0625
    o_ref[...] = out.astype(o_ref.dtype)


def low_pass(res, left, right, rows):
    tall, n_cols, ifg = res.shape
    whole = pl.BlockSpec(memory_space=pltpu.VMEM)
    return pl.pallas_call(
        filter_kernel,
        in_specs=[whole, whole, whole],
        out_specs=whole,
        out_shape=jax.ShapeDtypeStruct((rows, n_cols, ifg), jnp.bfloat16),
        scratch_shapes=[
            pltpu.VMEM((tall, n_cols + 2 * FILTER_HALO, ifg), jnp.float32),
            pltpu.VMEM((rows, n_cols + 2 * FILTER_HALO, ifg), jnp.float32),
        ],
        cost_estimate=pl.CostEstimate(
            flops=20 * tall * n_cols * ifg, bytes_accessed=6 * tall * n_cols * ifg, transcendentals=0
        ),
    )(res, left, right)


def binomial(padded, axis):
    length = padded.shape[axis] - 4

    def shifted(offset):
        return lax.slice_in_dim(padded, offset, offset + length, axis=axis)

    return (
        shifted(0) + 4.0 * shifted(1) + 6.0 * shifted(2) + 4.0 * shifted(3) + shifted(4)
    ) * 0.0625


def network_maps(network):
    date_ids = jnp.arange(DATES, dtype=jnp.int32)[None, :]
    full = (network[:, 1:2] == date_ids).astype(jnp.float32) - (network[:, 0:1] == date_ids).astype(
        jnp.float32
    )
    design = full[:, 1:]
    normal_matrix = jnp.dot(design.T, design, precision=lax.Precision.HIGHEST)
    factor = jnp.linalg.cholesky(normal_matrix)
    pseudo = jax.scipy.linalg.cho_solve((factor, True), design.T)
    return (design, pseudo)


def on_device(phase, weights, network):
    design, pseudo = network_maps(network)
    rows = phase.shape[1]
    count = lax.axis_size("rows")
    forward = [(i, i + 1) for i in range(count - 1)]
    backward = [(target, source) for source, target in forward]
    edge_low = jnp.stack([phase[:, rows - HALO :], weights[:, rows - HALO :].astype(jnp.float32)])
    edge_high = jnp.stack([phase[:, :HALO], weights[:, :HALO].astype(jnp.float32)])
    top = lax.ppermute(edge_low, "rows", forward)
    bottom = lax.ppermute(edge_high, "rows", backward)
    current = unwrap(phase, weights, top, bottom)
    received = lax.all_to_all(current, "ifg", split_axis=0, concat_axis=0, tiled=True)
    half = rows // 2 + FILTER_HALO
    series_t, residual_t = invert(received.reshape(-1, 128), pseudo, design, half)

    def unpack(x):
        return x.reshape(-1, 64, x.shape[1]).transpose(2, 0, 1)

    series_block = unpack(series_t)
    ifg = residual_t.shape[1]
    res = residual_t.reshape(-1, 64, ifg)
    count = lax.axis_size("ifg")
    forward = [(i, i + 1) for i in range(count - 1)]
    backward = [(target, source) for source, target in forward]
    left = lax.ppermute(res[:, 64 - FILTER_HALO :], "ifg", forward)
    right = lax.ppermute(res[:, :FILTER_HALO], "ifg", backward)
    filtered = low_pass(res, left, right, rows).transpose(2, 0, 1)
    return (series_block, filtered)


def solution(mesh):
    return jax.shard_map(
        on_device,
        mesh=mesh,
        in_specs=(P("ifg", "rows", None), P("ifg", "rows", None), P()),
        out_specs=(P(None, "rows", "ifg"), P(None, "rows", "ifg")),
        check_vma=False,
    )
```

```python
import functools

import numpy as np
import jax
import jax.numpy as jnp
from jax import lax
from jax.experimental import pallas as pl
from jax.experimental.pallas import tpu as pltpu
from jax.sharding import PartitionSpec as P

DATES = 96
SWEEPS = 4
FILTER_HALO = 2
HALO = 8
PI32 = float(np.float32(np.pi))
TWO_PI_HI = float(np.float32(2 * np.pi))
TWO_PI_LO = float(np.float32(2 * np.pi - np.float64(np.float32(2 * np.pi))))


def extended_2(block, sides, width):
    for axis, dim in sides:
        count = lax.axis_size(axis)
        forward = [(i, i + 1) for i in range(count - 1)]
        backward = [(target, source) for source, target in forward]
        low = lax.ppermute(
            lax.slice_in_dim(block, block.shape[dim] - width, None, axis=dim), axis, forward
        )
        high = lax.ppermute(lax.slice_in_dim(block, 0, width, axis=dim), axis, backward)
        block = jnp.concatenate([low, block, high], axis=dim)
    return block


def wrapped_diff(delta):
    above = (delta - TWO_PI_HI) - TWO_PI_LO
    below = (delta + TWO_PI_HI) + TWO_PI_LO
    return jnp.where(delta >= PI32, above, jnp.where(delta <= -PI32, below, delta))


def unwrap_kernel(rows_out, ph_ref, wt_ref, top_ref, bot_ref, o_ref, p_ref, q_ref, cur_ref):
    for b in range(ph_ref.shape[0]):
        p_ref[pl.ds(0, HALO), :] = top_ref[0, b]
        p_ref[pl.ds(HALO, rows_out), :] = ph_ref[b]
        p_ref[pl.ds(HALO + rows_out, HALO), :] = bot_ref[0, b]
        q_ref[pl.ds(0, HALO), :] = top_ref[1, b]
        q_ref[pl.ds(HALO, rows_out), :] = wt_ref[b].astype(jnp.float32)
        q_ref[pl.ds(HALO + rows_out, HALO), :] = bot_ref[1, b]
        p = p_ref[...]
        q = q_ref[...]
        nr, nc = p.shape
        row = lax.broadcasted_iota(jnp.int32, (nr, nc), 0)
        col = lax.broadcasted_iota(jnp.int32, (nr, nc), 1)
        zero = jnp.zeros((nr, nc), jnp.float32)
        p_dn = pltpu.roll(p, nr - 1, 0)
        q_dn = pltpu.roll(q, nr - 1, 0)
        g_dn = wrapped_diff(p_dn - p)
        w_dn = jnp.where(row < nr - 1, q_dn * q, zero)
        p_rt = pltpu.roll(p, nc - 1, 1)
        q_rt = pltpu.roll(q, nc - 1, 1)
        g_rt = wrapped_diff(p_rt - p)
        w_rt = jnp.where(col < nc - 1, q_rt * q, zero)
        g_up = pltpu.roll(g_dn, 1, 0)
        w_up = pltpu.roll(w_dn, 1, 0)
        g_lt = pltpu.roll(g_rt, 1, 1)
        w_lt = pltpu.roll(w_rt, 1, 1)
        den = ((w_up + w_dn) + w_lt) + w_rt
        den = jnp.where(den > 0.0, den, 1.0)
        inv = 1.0 / den
        num = w_up * g_up
        num = num - w_dn * g_dn
        num = num + w_lt * g_lt
        num = num - w_rt * g_rt
        const = num * inv
        a_up, a_dn, a_lt, a_rt = w_up * inv, w_dn * inv, w_lt * inv, w_rt * inv
        cur = const
        for _ in range(SWEEPS - 1):
            nxt = const + a_up * pltpu.roll(cur, 1, 0)
            nxt = nxt + a_dn * pltpu.roll(cur, nr - 1, 0)
            nxt = nxt + a_lt * pltpu.roll(cur, 1, 1)
            nxt = nxt + a_rt * pltpu.roll(cur, nc - 1, 1)
            cur = nxt
        cur_ref[...] = cur
        half = rows_out // 2 + FILTER_HALO
        upper = cur_ref[pl.ds(HALO - FILTER_HALO, half), :]
        lower = cur_ref[pl.ds(HALO - FILTER_HALO + half, half), :]
        lane = lax.broadcasted_iota(jnp.int32, (half, nc), 1) % 128
        first = lane < 64
        even = jnp.where(first, upper, pltpu.roll(lower, 64, 1))
        odd = jnp.where(first, pltpu.roll(upper, nc - 64, 1), lower)
        for m in range(nc // 128):
            o_ref[2 * m, pl.ds(b * half, half), :] = even[:, 128 * m : 128 * (m + 1)]
            o_ref[2 * m + 1, pl.ds(b * half, half), :] = odd[:, 128 * m : 128 * (m + 1)]


def unwrap(phase, weights, top, bottom):
    n, rows_out, nc = phase.shape
    nr = rows_out + 2 * HALO
    per = 4
    half = rows_out // 2 + FILTER_HALO
    halo_spec = pl.BlockSpec((2, per, HALO, nc), lambda i: (0, i, 0, 0))
    return pl.pallas_call(
        functools.partial(unwrap_kernel, rows_out),
        grid=(n // per,),
        in_specs=[
            pl.BlockSpec((per, rows_out, nc), lambda i: (i, 0, 0)),
            pl.BlockSpec((per, rows_out, nc), lambda i: (i, 0, 0)),
            halo_spec,
            halo_spec,
        ],
        out_specs=pl.BlockSpec((nc // 64, per * half, 128), lambda i: (0, i, 0)),
        out_shape=jax.ShapeDtypeStruct((nc // 64, n * half, 128), jnp.float32),
        scratch_shapes=[pltpu.VMEM((nr, nc), jnp.float32)] * 3,
        cost_estimate=pl.CostEstimate(
            flops=120 * n * nr * nc, bytes_accessed=4 * n * nc * (2 * nr + rows_out), transcendentals=0
        ),
    )(phase, weights, top, bottom)


def invert_kernel(rows, x_ref, pseudo_in, design_in, s_ref, r_ref, pseudo_ref, design_ref):
    ifg = pseudo_ref.shape[1]
    own = rows - FILTER_HALO
    epochs = pseudo_in.shape[0]
    pseudo_ref[...] = jnp.zeros(pseudo_ref.shape, jnp.float32)
    design_ref[...] = jnp.zeros(design_ref.shape, jnp.float32)
    pseudo_ref[pl.ds(0, epochs), :] = pseudo_in[...]
    design_ref[:, pl.ds(0, epochs)] = design_in[...]
    pseudo = pseudo_ref[...]
    design_b = design_ref[...].astype(jnp.bfloat16)
    for k in range(rows):
        x = x_ref[pl.ds(k, ifg, stride=rows), :]
        series = jnp.dot(pseudo, x, precision=lax.Precision.HIGH, preferred_element_type=jnp.float32)
        series_hi = series.astype(jnp.bfloat16)
        series_lo = (series - series_hi.astype(jnp.float32)).astype(jnp.bfloat16)
        fit = jnp.dot(design_b, series_hi, preferred_element_type=jnp.float32)
        fit = fit + jnp.dot(design_b, series_lo, preferred_element_type=jnp.float32)
        res_t = (x - fit).T
        ser_t = series.T
        r_ref[pl.ds(k * 64, 64), :] = res_t[:64]
        r_ref[pl.ds((k + rows) * 64, 64), :] = res_t[64:]
        if k >= FILTER_HALO:
            s_ref[pl.ds((k - FILTER_HALO) * 64, 64), :] = ser_t[:64]
        if k < own:
            s_ref[pl.ds((k + own) * 64, 64), :] = ser_t[64:]


def invert(packed, pseudo, design, rows):
    ifg = pseudo.shape[1]
    epochs = pseudo.shape[0]
    wide = epochs + (-epochs) % 8
    whole = pl.BlockSpec(memory_space=pltpu.VMEM)
    series_t, residual_t = pl.pallas_call(
        functools.partial(invert_kernel, rows),
        in_specs=[whole, whole, whole],
        out_specs=(whole, whole),
        scratch_shapes=[pltpu.VMEM((wide, ifg), jnp.float32), pltpu.VMEM((ifg, wide), jnp.float32)],
        out_shape=(
            jax.ShapeDtypeStruct((2 * (rows - FILTER_HALO) * 64, wide), jnp.float32),
            jax.ShapeDtypeStruct((2 * rows * 64, ifg), jnp.float32),
        ),
        cost_estimate=pl.CostEstimate(
            flops=4 * 6 * wide * ifg * rows * 128,
            bytes_accessed=4 * 128 * rows * (2 * ifg + wide),
            transcendentals=0,
        ),
    )(packed, pseudo, design)
    return series_t[:, :epochs], residual_t


def binomial(padded, axis):
    length = padded.shape[axis] - 4

    def shifted(offset):
        return lax.slice_in_dim(padded, offset, offset + length, axis=axis)

    return (
        shifted(0) + 4.0 * shifted(1) + 6.0 * shifted(2) + 4.0 * shifted(3) + shifted(4)
    ) * 0.0625


def network_maps(network):
    date_ids = jnp.arange(DATES, dtype=jnp.int32)[None, :]
    full = (network[:, 1:2] == date_ids).astype(jnp.float32) - (network[:, 0:1] == date_ids).astype(
        jnp.float32
    )
    design = full[:, 1:]
    normal_matrix = jnp.dot(design.T, design, precision=lax.Precision.HIGHEST)
    factor = jnp.linalg.cholesky(normal_matrix)
    pseudo = jax.scipy.linalg.cho_solve((factor, True), design.T)
    return (design, pseudo)


def on_device(phase, weights, network):
    design, pseudo = network_maps(network)
    rows = phase.shape[1]
    count = lax.axis_size("rows")
    forward = [(i, i + 1) for i in range(count - 1)]
    backward = [(target, source) for source, target in forward]
    edge_low = jnp.stack([phase[:, rows - HALO :], weights[:, rows - HALO :].astype(jnp.float32)])
    edge_high = jnp.stack([phase[:, :HALO], weights[:, :HALO].astype(jnp.float32)])
    top = lax.ppermute(edge_low, "rows", forward)
    bottom = lax.ppermute(edge_high, "rows", backward)
    current = unwrap(phase, weights, top, bottom)
    received = lax.all_to_all(current, "ifg", split_axis=0, concat_axis=0, tiled=True)
    half = rows // 2 + FILTER_HALO
    series_t, residual_t = invert(received.reshape(-1, 128), pseudo, design, half)

    def unpack(x):
        return x.reshape(-1, 64, x.shape[1]).transpose(2, 0, 1)

    series_block = unpack(series_t)
    residual = unpack(residual_t)
    padded = extended_2(residual, (("ifg", 2),), FILTER_HALO)
    filtered = binomial(binomial(padded, 1), 2)
    return (series_block, filtered.astype(jnp.bfloat16))


def solution(mesh):
    return jax.shard_map(
        on_device,
        mesh=mesh,
        in_specs=(P("ifg", "rows", None), P("ifg", "rows", None), P()),
        out_specs=(P(None, "rows", "ifg"), P(None, "rows", "ifg")),
        check_vma=False,
    )
```

```python
import functools

import numpy as np
import jax
import jax.numpy as jnp
from jax import lax
from jax.experimental import pallas as pl
from jax.experimental.pallas import tpu as pltpu
from jax.sharding import PartitionSpec as P

DATES = 96
SWEEPS = 4
FILTER_HALO = 2
SENT = SWEEPS + FILTER_HALO
HALO = 8
PI32 = float(np.float32(np.pi))
TWO_PI_HI = float(np.float32(2 * np.pi))
TWO_PI_LO = float(np.float32(2 * np.pi - np.float64(np.float32(2 * np.pi))))


def extended_2(block, sides, width):
    for axis, dim in sides:
        count = lax.axis_size(axis)
        forward = [(i, i + 1) for i in range(count - 1)]
        backward = [(target, source) for source, target in forward]
        low = lax.ppermute(
            lax.slice_in_dim(block, block.shape[dim] - width, None, axis=dim), axis, forward
        )
        high = lax.ppermute(lax.slice_in_dim(block, 0, width, axis=dim), axis, backward)
        block = jnp.concatenate([low, block, high], axis=dim)
    return block


def wrapped_diff(delta):
    above = (delta - TWO_PI_HI) - TWO_PI_LO
    below = (delta + TWO_PI_HI) + TWO_PI_LO
    return jnp.where(delta >= PI32, above, jnp.where(delta <= -PI32, below, delta))


def unwrap_kernel(rows_out, ph_ref, wt_ref, top_ref, bot_ref, o_ref, p_ref, q_ref, cur_ref):
    for b in range(ph_ref.shape[0]):
        spare = HALO - SENT
        blank = jnp.zeros((spare, p_ref.shape[1]), jnp.float32)
        for ref in (p_ref, q_ref):
            ref[pl.ds(0, spare), :] = blank
            ref[pl.ds(HALO + rows_out + SENT, spare), :] = blank
        p_ref[pl.ds(spare, SENT), :] = top_ref[0, b]
        p_ref[pl.ds(HALO, rows_out), :] = ph_ref[b]
        p_ref[pl.ds(HALO + rows_out, SENT), :] = bot_ref[0, b]
        q_ref[pl.ds(spare, SENT), :] = top_ref[1, b]
        q_ref[pl.ds(HALO, rows_out), :] = wt_ref[b].astype(jnp.float32)
        q_ref[pl.ds(HALO + rows_out, SENT), :] = bot_ref[1, b]
        p = p_ref[...]
        q = q_ref[...]
        nr, nc = p.shape
        row = lax.broadcasted_iota(jnp.int32, (nr, nc), 0)
        col = lax.broadcasted_iota(jnp.int32, (nr, nc), 1)
        zero = jnp.zeros((nr, nc), jnp.float32)
        p_dn = pltpu.roll(p, nr - 1, 0)
        q_dn = pltpu.roll(q, nr - 1, 0)
        g_dn = wrapped_diff(p_dn - p)
        w_dn = jnp.where(row < nr - 1, q_dn * q, zero)
        p_rt = pltpu.roll(p, nc - 1, 1)
        q_rt = pltpu.roll(q, nc - 1, 1)
        g_rt = wrapped_diff(p_rt - p)
        w_rt = jnp.where(col < nc - 1, q_rt * q, zero)
        g_up = pltpu.roll(g_dn, 1, 0)
        w_up = pltpu.roll(w_dn, 1, 0)
        g_lt = pltpu.roll(g_rt, 1, 1)
        w_lt = pltpu.roll(w_rt, 1, 1)
        den = ((w_up + w_dn) + w_lt) + w_rt
        den = jnp.where(den > 0.0, den, 1.0)
        inv = 1.0 / den
        num = w_up * g_up
        num = num - w_dn * g_dn
        num = num + w_lt * g_lt
        num = num - w_rt * g_rt
        const = num * inv
        a_up, a_dn, a_lt, a_rt = w_up * inv, w_dn * inv, w_lt * inv, w_rt * inv
        cur = const
        for _ in range(SWEEPS - 1):
            nxt = const + a_up * pltpu.roll(cur, 1, 0)
            nxt = nxt + a_dn * pltpu.roll(cur, nr - 1, 0)
            nxt = nxt + a_lt * pltpu.roll(cur, 1, 1)
            nxt = nxt + a_rt * pltpu.roll(cur, nc - 1, 1)
            cur = nxt
        cur_ref[...] = cur
        half = rows_out // 2 + FILTER_HALO
        upper = cur_ref[pl.ds(HALO - FILTER_HALO, half), :]
        lower = cur_ref[pl.ds(HALO - FILTER_HALO + half, half), :]
        lane = lax.broadcasted_iota(jnp.int32, (half, nc), 1) % 128
        first = lane < 64
        even = jnp.where(first, upper, pltpu.roll(lower, 64, 1))
        odd = jnp.where(first, pltpu.roll(upper, nc - 64, 1), lower)
        for m in range(nc // 128):
            o_ref[2 * m, pl.ds(b * half, half), :] = even[:, 128 * m : 128 * (m + 1)]
            o_ref[2 * m + 1, pl.ds(b * half, half), :] = odd[:, 128 * m : 128 * (m + 1)]


def unwrap(phase, weights, top, bottom):
    n, rows_out, nc = phase.shape
    nr = rows_out + 2 * HALO
    per = 4
    half = rows_out // 2 + FILTER_HALO
    halo_spec = pl.BlockSpec((2, per, SENT, nc), lambda i: (0, i, 0, 0))
    return pl.pallas_call(
        functools.partial(unwrap_kernel, rows_out),
        grid=(n // per,),
        in_specs=[
            pl.BlockSpec((per, rows_out, nc), lambda i: (i, 0, 0)),
            pl.BlockSpec((per, rows_out, nc), lambda i: (i, 0, 0)),
            halo_spec,
            halo_spec,
        ],
        out_specs=pl.BlockSpec((nc // 64, per * half, 128), lambda i: (0, i, 0)),
        out_shape=jax.ShapeDtypeStruct((nc // 64, n * half, 128), jnp.float32),
        scratch_shapes=[pltpu.VMEM((nr, nc), jnp.float32)] * 3,
        cost_estimate=pl.CostEstimate(
            flops=120 * n * nr * nc, bytes_accessed=4 * n * nc * (2 * nr + rows_out), transcendentals=0
        ),
    )(phase, weights, top, bottom)


def invert_kernel(rows, x_ref, pseudo_in, design_in, s_ref, r_ref, pseudo_ref, design_ref):
    ifg = pseudo_ref.shape[1]
    own = rows - FILTER_HALO
    epochs = pseudo_in.shape[0]
    pseudo_ref[...] = jnp.zeros(pseudo_ref.shape, jnp.float32)
    design_ref[...] = jnp.zeros(design_ref.shape, jnp.float32)
    pseudo_ref[pl.ds(0, epochs), :] = pseudo_in[...]
    design_ref[:, pl.ds(0, epochs)] = design_in[...]
    pseudo = pseudo_ref[...]
    design = design_ref[...]
    for k in range(rows):
        x = x_ref[pl.ds(k, ifg, stride=rows), :]
        series = jnp.dot(pseudo, x, precision=lax.Precision.HIGH, preferred_element_type=jnp.float32)
        fit = jnp.dot(design, series, precision=lax.Precision.HIGH, preferred_element_type=jnp.float32)
        res_t = (x - fit).T
        ser_t = series.T
        r_ref[pl.ds(k * 64, 64), :] = res_t[:64]
        r_ref[pl.ds((k + rows) * 64, 64), :] = res_t[64:]
        if k >= FILTER_HALO:
            s_ref[pl.ds((k - FILTER_HALO) * 64, 64), :] = ser_t[:64]
        if k < own:
            s_ref[pl.ds((k + own) * 64, 64), :] = ser_t[64:]


def invert(packed, pseudo, design, rows):
    ifg = pseudo.shape[1]
    epochs = pseudo.shape[0]
    wide = epochs + (-epochs) % 8
    whole = pl.BlockSpec(memory_space=pltpu.VMEM)
    series_t, residual_t = pl.pallas_call(
        functools.partial(invert_kernel, rows),
        in_specs=[whole, whole, whole],
        out_specs=(whole, whole),
        scratch_shapes=[pltpu.VMEM((wide, ifg), jnp.float32), pltpu.VMEM((ifg, wide), jnp.float32)],
        out_shape=(
            jax.ShapeDtypeStruct((2 * (rows - FILTER_HALO) * 64, wide), jnp.float32),
            jax.ShapeDtypeStruct((2 * rows * 64, ifg), jnp.float32),
        ),
        cost_estimate=pl.CostEstimate(
            flops=4 * 6 * wide * ifg * rows * 128,
            bytes_accessed=4 * 128 * rows * (2 * ifg + wide),
            transcendentals=0,
        ),
    )(packed, pseudo, design)
    return series_t[:, :epochs], residual_t


def binomial(padded, axis):
    length = padded.shape[axis] - 4

    def shifted(offset):
        return lax.slice_in_dim(padded, offset, offset + length, axis=axis)

    return (
        shifted(0) + 4.0 * shifted(1) + 6.0 * shifted(2) + 4.0 * shifted(3) + shifted(4)
    ) * 0.0625


def network_maps(network):
    date_ids = jnp.arange(DATES, dtype=jnp.int32)[None, :]
    full = (network[:, 1:2] == date_ids).astype(jnp.float32) - (network[:, 0:1] == date_ids).astype(
        jnp.float32
    )
    design = full[:, 1:]
    normal_matrix = jnp.dot(design.T, design, precision=lax.Precision.HIGHEST)
    factor = jnp.linalg.cholesky(normal_matrix)
    pseudo = jax.scipy.linalg.cho_solve((factor, True), design.T)
    return (design, pseudo)


def on_device(phase, weights, network):
    design, pseudo = network_maps(network)
    rows = phase.shape[1]
    count = lax.axis_size("rows")
    forward = [(i, i + 1) for i in range(count - 1)]
    backward = [(target, source) for source, target in forward]
    edge_low = jnp.stack([phase[:, rows - SENT :], weights[:, rows - SENT :].astype(jnp.float32)])
    edge_high = jnp.stack([phase[:, :SENT], weights[:, :SENT].astype(jnp.float32)])
    top = lax.ppermute(edge_low, "rows", forward)
    bottom = lax.ppermute(edge_high, "rows", backward)
    current = unwrap(phase, weights, top, bottom)
    received = lax.all_to_all(current, "ifg", split_axis=0, concat_axis=0, tiled=True)
    half = rows // 2 + FILTER_HALO
    series_t, residual_t = invert(received.reshape(-1, 128), pseudo, design, half)

    def unpack(x):
        return x.reshape(-1, 64, x.shape[1]).transpose(2, 0, 1)

    series_block = unpack(series_t)
    residual = unpack(residual_t)
    padded = extended_2(residual, (("ifg", 2),), FILTER_HALO)
    filtered = binomial(binomial(padded, 1), 2)
    return (series_block, filtered.astype(jnp.bfloat16))


def solution(mesh):
    return jax.shard_map(
        on_device,
        mesh=mesh,
        in_specs=(P("ifg", "rows", None), P("ifg", "rows", None), P()),
        out_specs=(P(None, "rows", "ifg"), P(None, "rows", "ifg")),
        check_vma=False,
    )
```
